128 devices in a mesh: role: 2 (over core), dev: 64 (over z, y, x).
Axes of the slice: x: 4, y: 4, z: 4, core: 2. Of those that a mesh axis runs over, the one named last changes fastest.
Arguments:
- moe_rows: bfloat16 [4096, 3584], P(('role', 'dev')), may hold values from -6 to 6
- expert_ids: int32 [4096, 8], P(('role', 'dev')), may hold values from 0 to 63, all different within a row; in each aligned block of 32 rows (0 to 31, 32 to 63, ...) at most 8 rows name the same one
- gate_weights: float32 [4096, 8], P(('role', 'dev')), may hold values from 0.05 to 0.6
- w_gate: bfloat16 [64, 3584, 1024], P('dev', None, 'role'), may hold values from -0.09375 to 0.09375
- w_up: bfloat16 [64, 3584, 1024], P('dev', None, 'role'), may hold values from -0.09375 to 0.09375
- w_down: bfloat16 [64, 3584, 1024], P('dev', None, 'role'), may hold values from -0.1875 to 0.1875
- q_latent: bfloat16 [512, 64, 512], P(('role', 'dev')), may hold values from -40 to 40
- q_rope: bfloat16 [512, 4096], P(('role', 'dev')), may hold values from -4 to 4
- latent_cache: bfloat16 [512, 2048, 512], P(('role', 'dev')), may hold values from -4 to 4
- rope_cache: bfloat16 [512, 64, 2048], P(('role', 'dev')), may hold values from -4 to 4
- lengths: int32 [512], P(('role', 'dev')), may hold values from 2 to 2048, as said below
Outputs:
- moe_out: bfloat16 [4096, 3584], P(('role', 'dev'))
- attended: bfloat16 [512, 64, 512], P(('role', 'dev'))
The draws below stay inside these ranges and needn't reach their ends.
Inputs may be any that keep to these rules, and one draw needn't show every extreme that they name: `expert_ids`: each row names 8 different experts; among the rows of one device no expert is named more than 8 times. `lengths`: the first row holds all 2048 cached tokens.
All inputs are finite; a program needn't handle non-finite values.
Results may differ from the reference program's by a relative error of at most 0.0057.
Values may be sent and summed in bfloat16 or wider, within the bound.
A program may use at most 128 MiB of HBM per device.

```python
import math
import jax
import jax.numpy as jnp
import numpy as np
from jax import lax

DW = 3584
FFW = 1024
TOPK = 8
HEADS = 64
LATENT = 512
ROPE = 64
TOK_DEV = 32
CACHE = 2048
EXPERTS = 64
CAP = 8
ROWS_MOE = 4096
ROWS_ATT = 512
N_ROLE = 2
N_DEV = 64


def cache_field(key):
    base = jnp.clip(jax.random.normal(jax.random.fold_in(key, 7), (ROWS_ATT, CACHE, LATENT), jnp.float32), -4.0, 4.0)
    return base


def draw_latent_cache(key, part):
    return cache_field(key).astype(jnp.bfloat16)


def draw_q_latent(key, part):
    result = jnp.clip(jax.random.normal(jax.random.fold_in(key, 19), (ROWS_ATT, HEADS, LATENT), jnp.float32), -4.0, 4.0)
    return result.astype(jnp.bfloat16)


def draw_q_rope(key, part):
    result = jnp.clip(jax.random.normal(jax.random.fold_in(key, 23), (ROWS_ATT, HEADS * ROPE), jnp.float32), -4.0, 4.0)
    return result.astype(jnp.bfloat16)


def draw_lengths(key, part):
    drawn = jax.random.randint(jax.random.fold_in(key, 29), (ROWS_ATT,), 2, CACHE + 1, jnp.int32)
    return jnp.where(jnp.arange(ROWS_ATT) == 0, CACHE, drawn).astype(jnp.int32)


def steps_of(key, extent, split, smallest, high):
    loudness, own = 1.0, jax.random.fold_in(key, 6)
    for axis_at, parts in split:
        draws = jnp.exp(jax.random.uniform(jax.random.fold_in(own, axis_at), (parts,), jnp.float32, smallest / len(split), high / len(split)))
        loudness = loudness * jnp.repeat(draws, extent[axis_at] // parts).reshape([-1 if axis == axis_at else 1 for axis in range(len(extent))])
    return loudness


def deal_out(own_key, own, number, rows, amount, top, most, skew):
    order = jax.random.permutation(own_key, amount)
    packed, usual = portions_of(amount, rows * top, most, skew, True), portions_of(amount, rows * top, most, skew, False)
    places = jnp.arange(amount)

    def named(sizes, offset_by):
        used = int((sizes > 0).sum())
        fixed = max(1, used // 4)
        passed = fixed + (places - fixed + offset_by * (used - fixed)) % max(1, amount - fixed)
        return jnp.zeros((amount,), jnp.int32).at[order[jnp.where(places < fixed, places, passed)]].set(jnp.asarray(sizes, jnp.int32))

    sizes = jnp.where(number % 4 == 0, named(packed, number // 4), named(usual, number - number // 4 - 1))
    mixed = jax.random.permutation(jax.random.fold_in(own, 3), amount)
    giver, taker = mixed[0:amount // 2 * 2:2], mixed[1:amount // 2 * 2:2]
    margin = jnp.minimum(sizes[giver] - 1, most - sizes[taker]) // 2
    margin = jnp.where((giver == order[0]) | (taker == order[0]) | (sizes[taker] == 0), 0, jnp.maximum(margin, 0))
    passed = jax.random.randint(jax.random.fold_in(own, 4), (amount // 2,), 0, 1 << 20) % (margin + 1)
    sizes = sizes.at[giver].add(-passed).at[taker].add(passed)
    items = jnp.searchsorted(jnp.cumsum(sizes), jnp.arange(rows * top), side="right").astype(jnp.int32)
    table = items.reshape(top, rows).T
    table = table[jax.random.permutation(jax.random.fold_in(own, 1), rows)]
    offset_by = jax.random.randint(jax.random.fold_in(own, 2), (rows, 1), 0, top)
    return jnp.take_along_axis(table, (jnp.arange(top)[None, :] + offset_by) % top, axis=1)


def portions_of(amount, total, reach, slope, full):
    loads = [(1 << 20) // math.isqrt(grade ** slope) + 1 for grade in range(1, amount + 1)]
    largest = reach if full else min(reach, max(-(-total // amount), total * loads[0] // sum(loads)))
    least = 1 if total - largest >= amount - 1 else 0
    given, surplus = [largest] + [least] * (amount - 1), total - largest - least * (amount - 1)
    while surplus > 0:
        movable = [i for i in range(1, amount) if given[i] < largest] or [i for i in range(1, amount) if given[i] < reach]
        whole, remaining = sum([loads[i] for i in movable]), surplus
        for i in movable:
            extra = min(reach - given[i], max(1, remaining * loads[i] // whole), surplus)
            given[i] = given[i] + extra
            surplus = surplus - extra
    return np.array(given)


def gaussian(rng, extent, spread, most, shards=(), kind=jnp.bfloat16):
    array = jax.random.normal(rng, extent, jnp.float32) * spread
    if len(shards) > 0:
        array = steps_of(rng, extent, shards, -0.22, 0.18) * array
    return jnp.clip(array, min=-most, max=most).astype(kind)


def setup_inputs(seed: int = 0) -> dict:
    key_list = jax.random.split(jax.random.key(seed), 12)
    moe_rows = gaussian(key_list[0], (ROWS_MOE, DW), 1.0, 6.0, ((0, 128),))
    expert_ids_keys = jax.random.split(jax.random.fold_in(key_list[1], 1), ROWS_MOE // TOK_DEV)
    expert_ids_turns = jax.random.permutation(jax.random.fold_in(key_list[1], 3), ROWS_MOE // TOK_DEV)
    expert_ids = jax.vmap(lambda own, number: deal_out(jax.random.fold_in(key_list[1], 2), own, number, TOK_DEV, EXPERTS, TOPK, CAP, 2))(expert_ids_keys, expert_ids_turns).reshape((ROWS_MOE, TOPK))
    gate_weights = jnp.clip(0.05 + 0.55 * jax.random.uniform(key_list[2], (ROWS_MOE, TOPK), jnp.float32) ** steps_of(key_list[2], (ROWS_MOE, TOPK), ((0, 128),), -0.2, 0.2), 0.05, 0.6)
    w_gate = gaussian(key_list[3], (EXPERTS, DW, FFW), DW ** -0.5, 0.09375, ((0, 64), (2, 2)))
    w_up = gaussian(key_list[4], (EXPERTS, DW, FFW), DW ** -0.5, 0.09375, ((0, 64), (2, 2)))
    w_down = gaussian(key_list[5], (EXPERTS, DW, FFW), FFW ** -0.5, 0.1875, ((0, 64), (2, 2)))
    q_latent = draw_q_latent(jax.random.fold_in(key_list[11], 71), 0)
    q_rope = draw_q_rope(jax.random.fold_in(key_list[11], 71), 0)
    latent_cache = draw_latent_cache(jax.random.fold_in(key_list[11], 71), 0)
    rope_cache = gaussian(key_list[9], (ROWS_ATT, ROPE, CACHE), 1.0, 4.0, ((0, 128),))
    lengths = draw_lengths(jax.random.fold_in(key_list[11], 71), 0)
    return {"moe_rows": moe_rows, "expert_ids": expert_ids, "gate_weights": gate_weights, "w_gate": w_gate, "w_up": w_up, "w_down": w_down, "q_latent": q_latent, "q_rope": q_rope, "latent_cache": latent_cache, "rope_cache": rope_cache, "lengths": lengths}


score_scale = 192.0 ** -0.5


def expert_block(chosen, gate_matrix, up_matrix, down_matrix):
    gate_part = jnp.dot(chosen, gate_matrix, preferred_element_type=jnp.float32)
    up_part = jnp.dot(chosen, up_matrix, preferred_element_type=jnp.float32)
    hidden_units = (jax.nn.silu(gate_part) * up_part).astype(jnp.bfloat16)
    return lax.dot_general(hidden_units, down_matrix, (((1,), (1,)), ((), ())), preferred_element_type=jnp.float32)


def attend_row(operands):
    query_lat, query_rope, cache_lat, cache_rope, length = operands
    head_count = query_lat.shape[0]
    rope_width = cache_rope.shape[0]
    scores = lax.dot_general(query_lat, cache_lat, (((1,), (1,)), ((), ())), preferred_element_type=jnp.float32)
    scores = scores + jnp.dot(query_rope.reshape(head_count, rope_width), cache_rope, preferred_element_type=jnp.float32)
    scores = scores * score_scale
    positions = jnp.arange(cache_lat.shape[0], dtype=jnp.int32)
    valid = (positions < length)[None, :]
    scores = jnp.where(valid, scores, jnp.float32(-1e30))
    highest = jnp.max(scores, axis=1, keepdims=True)
    weights = jnp.where(valid, jnp.exp(scores - highest), jnp.float32(0.0))
    probs = (weights / jnp.sum(weights, axis=1, keepdims=True)).astype(jnp.bfloat16)
    return jnp.dot(probs, cache_lat, preferred_element_type=jnp.float32).astype(jnp.bfloat16)


def reference(moe_rows, expert_ids, gate_weights, w_gate, w_up, w_down, q_latent, q_rope, latent_cache, rope_cache, lengths):
    flat_ids = expert_ids.reshape(-1)
    pair_count = flat_ids.shape[0]
    width = moe_rows.shape[1]
    padded_rows = jnp.concatenate([moe_rows, jnp.zeros((1, width), jnp.bfloat16)], axis=0)
    flat_gates = jnp.concatenate([gate_weights.reshape(-1), jnp.zeros((1,), jnp.float32)], axis=0)
    bound = N_ROLE * N_DEV * CAP

    def per_expert(running, expert):
        picks = jnp.nonzero(flat_ids == expert, size=bound, fill_value=pair_count)[0].astype(jnp.int32)
        row_index = jnp.where(picks < pair_count, picks // TOPK, ROWS_MOE).astype(jnp.int32)
        chosen = padded_rows[row_index]
        result = expert_block(chosen, w_gate[expert], w_up[expert], w_down[expert]).astype(jnp.bfloat16)
        result = lax.optimization_barrier(result).astype(jnp.float32)
        weighted = result * flat_gates[picks][:, None]
        return running.at[row_index].add(weighted), None

    start_sum = jnp.zeros((ROWS_MOE + 1, width), jnp.float32)
    running, _ = lax.scan(per_expert, start_sum, jnp.arange(EXPERTS, dtype=jnp.int32))
    moe_out = running[:ROWS_MOE].astype(jnp.bfloat16)
    attended = lax.map(attend_row, (q_latent, q_rope, latent_cache, rope_cache, lengths))
    return (moe_out, attended)
```

```python
import jax
import jax.numpy as jnp
from jax import lax
from jax.sharding import PartitionSpec as P

score_scale = 192.0 ** (-0.5)


def expert_block(chosen, gate_matrix, up_matrix, down_matrix):
    gate_part = jnp.dot(chosen, gate_matrix, preferred_element_type=jnp.float32)
    up_part = jnp.dot(chosen, up_matrix, preferred_element_type=jnp.float32)
    hidden_units = (jax.nn.silu(gate_part) * up_part).astype(jnp.bfloat16)
    return lax.dot_general(
        hidden_units, down_matrix, (((1,), (1,)), ((), ())), preferred_element_type=jnp.float32
    )


def full_expert(rows, w_gate, w_up, w_down):
    gate_both = lax.all_gather(w_gate[0], "role", axis=0)
    up_both = lax.all_gather(w_up[0], "role", axis=0)
    down_both = lax.all_gather(w_down[0], "role", axis=0)
    total = None
    for half in range(gate_both.shape[0]):
        gate_part = jnp.dot(rows, gate_both[half], preferred_element_type=jnp.float32)
        up_part = jnp.dot(rows, up_both[half], preferred_element_type=jnp.float32)
        hidden_units = (jax.nn.silu(gate_part) * up_part).astype(jnp.bfloat16)
        term = lax.dot_general(
            hidden_units, down_both[half], (((1,), (1,)), ((), ())), preferred_element_type=jnp.float32
        )
        total = term if total is None else total + term
    return total


def attend_row(query_lat, query_rope, cache_lat, cache_rope, length):
    head_count = query_lat.shape[0]
    rope_width = cache_rope.shape[0]
    scores = lax.dot_general(
        query_lat, cache_lat, (((1,), (1,)), ((), ())), preferred_element_type=jnp.float32
    )
    scores = scores + jnp.dot(
        query_rope.reshape(head_count, rope_width), cache_rope, preferred_element_type=jnp.float32
    )
    scores = scores * score_scale
    positions = jnp.arange(cache_lat.shape[0], dtype=jnp.int32)
    valid = (positions < length)[None, :]
    scores = jnp.where(valid, scores, jnp.float32(-1e30))
    highest = jnp.max(scores, axis=1, keepdims=True)
    weights = jnp.where(valid, jnp.exp(scores - highest), jnp.float32(0.0))
    probs = (weights / jnp.sum(weights, axis=1, keepdims=True)).astype(jnp.bfloat16)
    return jnp.dot(probs, cache_lat, preferred_element_type=jnp.float32).astype(jnp.bfloat16)


def per_device(
    moe_rows,
    expert_ids,
    gate_weights,
    w_gate,
    w_up,
    w_down,
    q_latent,
    q_rope,
    latent_cache,
    rope_cache,
    lengths,
):
    tok_count = moe_rows.shape[0]
    width = moe_rows.shape[1]
    topk_count = expert_ids.shape[1]
    experts = lax.axis_size("dev")
    capacity = min(tok_count, 2 * tok_count * topk_count // experts)
    flat_ids = expert_ids.reshape(-1)
    pair_count = flat_ids.shape[0]
    one_hot = (flat_ids[:, None] == jnp.arange(experts, dtype=jnp.int32)[None, :]).astype(jnp.int32)
    earlier = jnp.cumsum(one_hot, axis=0) - one_hot
    slot_index = jnp.sum(earlier * one_hot, axis=1)
    destination = flat_ids * capacity + slot_index
    source_row = jnp.full((experts * capacity,), tok_count, jnp.int32)
    source_row = source_row.at[destination].set(
        jnp.arange(pair_count, dtype=jnp.int32) // topk_count
    )
    padded_rows = jnp.concatenate([moe_rows, jnp.zeros((1, width), jnp.bfloat16)], axis=0)
    outgoing = padded_rows[source_row].reshape(experts, capacity, width)
    arrived = lax.all_to_all(outgoing, "dev", split_axis=0, concat_axis=0, tiled=True)
    own_rows = arrived.reshape(experts * capacity, width)
    expert_sum = full_expert(own_rows, w_gate, w_up, w_down)
    finished = expert_sum.astype(jnp.bfloat16).reshape(experts, capacity, width)
    returned = lax.all_to_all(finished, "dev", split_axis=0, concat_axis=0, tiled=True)
    flat_back = returned.reshape(experts * capacity, width)
    picked = flat_back[destination].reshape(tok_count, topk_count, width).astype(jnp.float32)
    moe_out = jnp.sum(picked * gate_weights[:, :, None], axis=1).astype(jnp.bfloat16)
    attended = jax.vmap(attend_row)(q_latent, q_rope, latent_cache, rope_cache, lengths)
    return (moe_out, attended)


def solution(mesh):
    placed = (
        P(("role", "dev"), None),
        P(("role", "dev"), None),
        P(("role", "dev"), None),
        P("dev", None, "role"),
        P("dev", None, "role"),
        P("dev", None, "role"),
        P(("role", "dev"), None, None),
        P(("role", "dev"), None),
        P(("role", "dev"), None, None),
        P(("role", "dev"), None, None),
        P(("role", "dev")),
    )
    return jax.shard_map(
        per_device,
        mesh=mesh,
        in_specs=placed,
        out_specs=(P(("role", "dev"), None), P(("role", "dev"), None, None)),
        check_vma=False,
    )
```

```python
import jax
import jax.numpy as jnp
from jax import lax
from jax.sharding import PartitionSpec as P
from jax.experimental import pallas as pl
from jax.experimental.pallas import tpu as pltpu
import functools

MESH = pl.DeviceIdType.MESH

def a2a_kernel(n, x_ref, o_ref, send_sems, recv_sems, local_sem):
    me = lax.axis_index("dev")
    core = lax.axis_index("role")
    local = pltpu.make_async_copy(x_ref.at[me], o_ref.at[me], local_sem)
    local.start()

    def describe(k):
        peer = lax.rem(me + k, n)
        return pltpu.make_async_remote_copy(
            src_ref=x_ref.at[peer],
            dst_ref=o_ref.at[me],
            send_sem=send_sems.at[k],
            recv_sem=recv_sems.at[k],
            device_id=(core, peer),
            device_id_type=MESH,
        )

    def issue(k, carry):
        describe(k).start()
        return carry

    lax.fori_loop(1, n, issue, 0)

    def finish(k, carry):
        describe(k).wait()
        return carry

    lax.fori_loop(1, n, finish, 0)
    local.wait()


def all_to_all_dev(x):
    n = lax.axis_size("dev")
    return pl.pallas_call(
        functools.partial(a2a_kernel, n),
        out_shape=jax.ShapeDtypeStruct(x.shape, x.dtype),
        in_specs=[pl.BlockSpec(memory_space=pl.ANY)],
        out_specs=pl.BlockSpec(memory_space=pl.ANY),
        scratch_shapes=[
            pltpu.SemaphoreType.DMA((n,)),
            pltpu.SemaphoreType.DMA((n,)),
            pltpu.SemaphoreType.DMA(()),
        ],
        compiler_params=pltpu.CompilerParams(has_side_effects=True),
    )(x)


score_scale = 192.0 ** (-0.5)


def expert_block(chosen, gate_matrix, up_matrix, down_matrix):
    gate_part = jnp.dot(chosen, gate_matrix, preferred_element_type=jnp.float32)
    up_part = jnp.dot(chosen, up_matrix, preferred_element_type=jnp.float32)
    hidden_units = (jax.nn.silu(gate_part) * up_part).astype(jnp.bfloat16)
    return lax.dot_general(
        hidden_units, down_matrix, (((1,), (1,)), ((), ())), preferred_element_type=jnp.float32
    )


def full_expert(rows, w_gate, w_up, w_down):
    gate_both = lax.all_gather(w_gate[0], "role", axis=0)
    up_both = lax.all_gather(w_up[0], "role", axis=0)
    down_both = lax.all_gather(w_down[0], "role", axis=0)
    total = None
    for half in range(gate_both.shape[0]):
        gate_part = jnp.dot(rows, gate_both[half], preferred_element_type=jnp.float32)
        up_part = jnp.dot(rows, up_both[half], preferred_element_type=jnp.float32)
        hidden_units = (jax.nn.silu(gate_part) * up_part).astype(jnp.bfloat16)
        term = lax.dot_general(
            hidden_units, down_both[half], (((1,), (1,)), ((), ())), preferred_element_type=jnp.float32
        )
        total = term if total is None else total + term
    return total


def attend_row(query_lat, query_rope, cache_lat, cache_rope, length):
    head_count = query_lat.shape[0]
    rope_width = cache_rope.shape[0]
    scores = lax.dot_general(
        query_lat, cache_lat, (((1,), (1,)), ((), ())), preferred_element_type=jnp.float32
    )
    scores = scores + jnp.dot(
        query_rope.reshape(head_count, rope_width), cache_rope, preferred_element_type=jnp.float32
    )
    scores = scores * score_scale
    positions = jnp.arange(cache_lat.shape[0], dtype=jnp.int32)
    valid = (positions < length)[None, :]
    scores = jnp.where(valid, scores, jnp.float32(-1e30))
    highest = jnp.max(scores, axis=1, keepdims=True)
    weights = jnp.where(valid, jnp.exp(scores - highest), jnp.float32(0.0))
    probs = (weights / jnp.sum(weights, axis=1, keepdims=True)).astype(jnp.bfloat16)
    return jnp.dot(probs, cache_lat, preferred_element_type=jnp.float32).astype(jnp.bfloat16)


def per_device(
    moe_rows,
    expert_ids,
    gate_weights,
    w_gate,
    w_up,
    w_down,
    q_latent,
    q_rope,
    latent_cache,
    rope_cache,
    lengths,
):
    tok_count = moe_rows.shape[0]
    width = moe_rows.shape[1]
    topk_count = expert_ids.shape[1]
    experts = lax.axis_size("dev")
    capacity = min(tok_count, 2 * tok_count * topk_count // experts)
    flat_ids = expert_ids.reshape(-1)
    pair_count = flat_ids.shape[0]
    one_hot = (flat_ids[:, None] == jnp.arange(experts, dtype=jnp.int32)[None, :]).astype(jnp.int32)
    earlier = jnp.cumsum(one_hot, axis=0) - one_hot
    slot_index = jnp.sum(earlier * one_hot, axis=1)
    destination = flat_ids * capacity + slot_index
    source_row = jnp.full((experts * capacity,), tok_count, jnp.int32)
    source_row = source_row.at[destination].set(
        jnp.arange(pair_count, dtype=jnp.int32) // topk_count
    )
    padded_rows = jnp.concatenate([moe_rows, jnp.zeros((1, width), jnp.bfloat16)], axis=0)
    outgoing = padded_rows[source_row].reshape(experts, capacity, width)
    arrived = all_to_all_dev(outgoing)
    own_rows = arrived.reshape(experts * capacity, width)
    expert_sum = full_expert(own_rows, w_gate, w_up, w_down)
    finished = expert_sum.astype(jnp.bfloat16).reshape(experts, capacity, width)
    returned = lax.all_to_all(finished, "dev", split_axis=0, concat_axis=0, tiled=True)
    flat_back = returned.reshape(experts * capacity, width)
    picked = flat_back[destination].reshape(tok_count, topk_count, width).astype(jnp.float32)
    moe_out = jnp.sum(picked * gate_weights[:, :, None], axis=1).astype(jnp.bfloat16)
    attended = jax.vmap(attend_row)(q_latent, q_rope, latent_cache, rope_cache, lengths)
    return (moe_out, attended)


def solution(mesh):
    placed = (
        P(("role", "dev"), None),
        P(("role", "dev"), None),
        P(("role", "dev"), None),
        P("dev", None, "role"),
        P("dev", None, "role"),
        P("dev", None, "role"),
        P(("role", "dev"), None, None),
        P(("role", "dev"), None),
        P(("role", "dev"), None, None),
        P(("role", "dev"), None, None),
        P(("role", "dev")),
    )
    return jax.shard_map(
        per_device,
        mesh=mesh,
        in_specs=placed,
        out_specs=(P(("role", "dev"), None), P(("role", "dev"), None, None)),
        check_vma=False,
    )
```

```python
import jax
import jax.numpy as jnp
from jax import lax
from jax.sharding import PartitionSpec as P
from jax.experimental import pallas as pl
from jax.experimental.pallas import tpu as pltpu
import functools

MESH = pl.DeviceIdType.MESH

def a2a_kernel(n, x_ref, o_ref, send_sems, recv_sems, local_sem):
    me = lax.axis_index("dev")
    core = lax.axis_index("role")
    local = pltpu.make_async_copy(x_ref.at[me], o_ref.at[me], local_sem)
    local.start()

    def offset_of(k):
        return lax.rem((k - 1) * 2 + me, n - 1) + 1

    def describe(offset):
        peer = lax.rem(me + offset, n)
        return pltpu.make_async_remote_copy(
            src_ref=x_ref.at[peer],
            dst_ref=o_ref.at[me],
            send_sem=send_sems.at[offset],
            recv_sem=recv_sems.at[offset],
            device_id=(core, peer),
            device_id_type=MESH,
        )

    def issue(k, carry):
        describe(offset_of(k)).start()
        return carry

    lax.fori_loop(1, n, issue, 0)

    def finish(offset, carry):
        describe(offset).wait()
        return carry

    lax.fori_loop(1, n, finish, 0)
    local.wait()


def all_to_all_dev(x):
    n = lax.axis_size("dev")
    return pl.pallas_call(
        functools.partial(a2a_kernel, n),
        out_shape=jax.ShapeDtypeStruct(x.shape, x.dtype),
        in_specs=[pl.BlockSpec(memory_space=pl.ANY)],
        out_specs=pl.BlockSpec(memory_space=pl.ANY),
        scratch_shapes=[
            pltpu.SemaphoreType.DMA((n,)),
            pltpu.SemaphoreType.DMA((n,)),
            pltpu.SemaphoreType.DMA(()),
        ],
        compiler_params=pltpu.CompilerParams(has_side_effects=True),
    )(x)


score_scale = 192.0 ** (-0.5)


def expert_block(chosen, gate_matrix, up_matrix, down_matrix):
    gate_part = jnp.dot(chosen, gate_matrix, preferred_element_type=jnp.float32)
    up_part = jnp.dot(chosen, up_matrix, preferred_element_type=jnp.float32)
    hidden_units = (jax.nn.silu(gate_part) * up_part).astype(jnp.bfloat16)
    return lax.dot_general(
        hidden_units, down_matrix, (((1,), (1,)), ((), ())), preferred_element_type=jnp.float32
    )


def full_expert(rows, w_gate, w_up, w_down):
    gate_both = lax.all_gather(w_gate[0], "role", axis=0)
    up_both = lax.all_gather(w_up[0], "role", axis=0)
    down_both = lax.all_gather(w_down[0], "role", axis=0)
    total = None
    for half in range(gate_both.shape[0]):
        gate_part = jnp.dot(rows, gate_both[half], preferred_element_type=jnp.float32)
        up_part = jnp.dot(rows, up_both[half], preferred_element_type=jnp.float32)
        hidden_units = (jax.nn.silu(gate_part) * up_part).astype(jnp.bfloat16)
        term = lax.dot_general(
            hidden_units, down_both[half], (((1,), (1,)), ((), ())), preferred_element_type=jnp.float32
        )
        total = term if total is None else total + term
    return total


def attend_row(query_lat, query_rope, cache_lat, cache_rope, length):
    head_count = query_lat.shape[0]
    rope_width = cache_rope.shape[0]
    scores = lax.dot_general(
        query_lat, cache_lat, (((1,), (1,)), ((), ())), preferred_element_type=jnp.float32
    )
    scores = scores + jnp.dot(
        query_rope.reshape(head_count, rope_width), cache_rope, preferred_element_type=jnp.float32
    )
    scores = scores * score_scale
    positions = jnp.arange(cache_lat.shape[0], dtype=jnp.int32)
    valid = (positions < length)[None, :]
    scores = jnp.where(valid, scores, jnp.float32(-1e30))
    highest = jnp.max(scores, axis=1, keepdims=True)
    weights = jnp.where(valid, jnp.exp(scores - highest), jnp.float32(0.0))
    probs = (weights / jnp.sum(weights, axis=1, keepdims=True)).astype(jnp.bfloat16)
    return jnp.dot(probs, cache_lat, preferred_element_type=jnp.float32).astype(jnp.bfloat16)


def per_device(
    moe_rows,
    expert_ids,
    gate_weights,
    w_gate,
    w_up,
    w_down,
    q_latent,
    q_rope,
    latent_cache,
    rope_cache,
    lengths,
):
    tok_count = moe_rows.shape[0]
    width = moe_rows.shape[1]
    topk_count = expert_ids.shape[1]
    experts = lax.axis_size("dev")
    capacity = min(tok_count, 2 * tok_count * topk_count // experts)
    flat_ids = expert_ids.reshape(-1)
    pair_count = flat_ids.shape[0]
    one_hot = (flat_ids[:, None] == jnp.arange(experts, dtype=jnp.int32)[None, :]).astype(jnp.int32)
    earlier = jnp.cumsum(one_hot, axis=0) - one_hot
    slot_index = jnp.sum(earlier * one_hot, axis=1)
    destination = flat_ids * capacity + slot_index
    source_row = jnp.full((experts * capacity,), tok_count, jnp.int32)
    source_row = source_row.at[destination].set(
        jnp.arange(pair_count, dtype=jnp.int32) // topk_count
    )
    padded_rows = jnp.concatenate([moe_rows, jnp.zeros((1, width), jnp.bfloat16)], axis=0)
    outgoing = padded_rows[source_row].reshape(experts, capacity, width)
    arrived = all_to_all_dev(outgoing)
    own_rows = arrived.reshape(experts * capacity, width)
    expert_sum = full_expert(own_rows, w_gate, w_up, w_down)
    finished = expert_sum.astype(jnp.bfloat16).reshape(experts, capacity, width)
    returned = lax.all_to_all(finished, "dev", split_axis=0, concat_axis=0, tiled=True)
    flat_back = returned.reshape(experts * capacity, width)
    picked = flat_back[destination].reshape(tok_count, topk_count, width).astype(jnp.float32)
    moe_out = jnp.sum(picked * gate_weights[:, :, None], axis=1).astype(jnp.bfloat16)
    attended = jax.vmap(attend_row)(q_latent, q_rope, latent_cache, rope_cache, lengths)
    return (moe_out, attended)


def solution(mesh):
    placed = (
        P(("role", "dev"), None),
        P(("role", "dev"), None),
        P(("role", "dev"), None),
        P("dev", None, "role"),
        P("dev", None, "role"),
        P("dev", None, "role"),
        P(("role", "dev"), None, None),
        P(("role", "dev"), None),
        P(("role", "dev"), None, None),
        P(("role", "dev"), None, None),
        P(("role", "dev")),
    )
    return jax.shard_map(
        per_device,
        mesh=mesh,
        in_specs=placed,
        out_specs=(P(("role", "dev"), None), P(("role", "dev"), None, None)),
        check_vma=False,
    )
```

```python
import jax
import jax.numpy as jnp
from jax import lax
from jax.sharding import PartitionSpec as P
from jax.experimental import pallas as pl
from jax.experimental.pallas import tpu as pltpu
import functools

def gate_up_kernel(x_ref, g_ref, u_ref, h_ref):
    x = x_ref[...]
    gate_part = jnp.dot(x, g_ref[0], preferred_element_type=jnp.float32)
    up_part = jnp.dot(x, u_ref[0], preferred_element_type=jnp.float32)
    h_ref[...] = (jax.nn.silu(gate_part) * up_part).astype(h_ref.dtype)


def down_kernel(halves, h_ref, d_ref, o_ref):
    width = d_ref.shape[2]
    total = None
    for half in range(halves):
        term = lax.dot_general(
            h_ref[:, half * width:(half + 1) * width],
            d_ref[half],
            (((1,), (1,)), ((), ())),
            preferred_element_type=jnp.float32,
        )
        total = term if total is None else total + term
    o_ref[...] = total.astype(o_ref.dtype)


def expert_ffn(rows, gate_both, up_both, down_both, unit_tile=256, out_tile=512):
    count, width = rows.shape
    halves, _, units = gate_both.shape
    steps = units // unit_tile
    hidden = pl.pallas_call(
        gate_up_kernel,
        out_shape=jax.ShapeDtypeStruct((count, halves * units), jnp.bfloat16),
        grid=(halves, steps),
        in_specs=[
            pl.BlockSpec((count, width), lambda c, j: (0, 0)),
            pl.BlockSpec((1, width, unit_tile), lambda c, j: (c, 0, j)),
            pl.BlockSpec((1, width, unit_tile), lambda c, j: (c, 0, j)),
        ],
        out_specs=pl.BlockSpec((count, unit_tile), lambda c, j: (0, c * steps + j)),
        compiler_params=pltpu.CompilerParams(vmem_limit_bytes=48 * 1024 * 1024),
        cost_estimate=pl.CostEstimate(
            flops=4 * count * width * halves * units,
            transcendentals=count * halves * units,
            bytes_accessed=2 * (count * width + 2 * width * halves * units + count * halves * units),
        ),
    )(rows, gate_both, up_both)
    out_steps = width // out_tile
    return pl.pallas_call(
        functools.partial(down_kernel, halves),
        out_shape=jax.ShapeDtypeStruct((count, width), jnp.bfloat16),
        grid=(out_steps,),
        in_specs=[
            pl.BlockSpec((count, halves * units), lambda j: (0, 0)),
            pl.BlockSpec((halves, out_tile, units), lambda j: (0, j, 0)),
        ],
        out_specs=pl.BlockSpec((count, out_tile), lambda j: (0, j)),
        compiler_params=pltpu.CompilerParams(vmem_limit_bytes=48 * 1024 * 1024),
        cost_estimate=pl.CostEstimate(
            flops=2 * count * width * halves * units,
            transcendentals=0,
            bytes_accessed=2 * (count * width + width * halves * units + count * halves * units),
        ),
    )(hidden, down_both)


score_scale = 192.0 ** (-0.5)


def expert_block(chosen, gate_matrix, up_matrix, down_matrix):
    gate_part = jnp.dot(chosen, gate_matrix, preferred_element_type=jnp.float32)
    up_part = jnp.dot(chosen, up_matrix, preferred_element_type=jnp.float32)
    hidden_units = (jax.nn.silu(gate_part) * up_part).astype(jnp.bfloat16)
    return lax.dot_general(
        hidden_units, down_matrix, (((1,), (1,)), ((), ())), preferred_element_type=jnp.float32
    )


def full_expert(rows, w_gate, w_up, w_down):
    gate_both = lax.all_gather(w_gate[0], "role", axis=0)
    up_both = lax.all_gather(w_up[0], "role", axis=0)
    down_both = lax.all_gather(w_down[0], "role", axis=0)
    return expert_ffn(rows, gate_both, up_both, down_both)


def attend_row(query_lat, query_rope, cache_lat, cache_rope, length):
    head_count = query_lat.shape[0]
    rope_width = cache_rope.shape[0]
    scores = lax.dot_general(
        query_lat, cache_lat, (((1,), (1,)), ((), ())), preferred_element_type=jnp.float32
    )
    scores = scores + jnp.dot(
        query_rope.reshape(head_count, rope_width), cache_rope, preferred_element_type=jnp.float32
    )
    scores = scores * score_scale
    positions = jnp.arange(cache_lat.shape[0], dtype=jnp.int32)
    valid = (positions < length)[None, :]
    scores = jnp.where(valid, scores, jnp.float32(-1e30))
    highest = jnp.max(scores, axis=1, keepdims=True)
    weights = jnp.where(valid, jnp.exp(scores - highest), jnp.float32(0.0))
    probs = (weights / jnp.sum(weights, axis=1, keepdims=True)).astype(jnp.bfloat16)
    return jnp.dot(probs, cache_lat, preferred_element_type=jnp.float32).astype(jnp.bfloat16)


def per_device(
    moe_rows,
    expert_ids,
    gate_weights,
    w_gate,
    w_up,
    w_down,
    q_latent,
    q_rope,
    latent_cache,
    rope_cache,
    lengths,
):
    tok_count = moe_rows.shape[0]
    width = moe_rows.shape[1]
    topk_count = expert_ids.shape[1]
    experts = lax.axis_size("dev")
    capacity = min(tok_count, 2 * tok_count * topk_count // experts)
    flat_ids = expert_ids.reshape(-1)
    pair_count = flat_ids.shape[0]
    one_hot = (flat_ids[:, None] == jnp.arange(experts, dtype=jnp.int32)[None, :]).astype(jnp.int32)
    earlier = jnp.cumsum(one_hot, axis=0) - one_hot
    slot_index = jnp.sum(earlier * one_hot, axis=1)
    destination = flat_ids * capacity + slot_index
    source_row = jnp.full((experts * capacity,), tok_count, jnp.int32)
    source_row = source_row.at[destination].set(
        jnp.arange(pair_count, dtype=jnp.int32) // topk_count
    )
    padded_rows = jnp.concatenate([moe_rows, jnp.zeros((1, width), jnp.bfloat16)], axis=0)
    outgoing = padded_rows[source_row].reshape(experts, capacity, width)
    arrived = lax.all_to_all(outgoing, "dev", split_axis=0, concat_axis=0, tiled=True)
    own_rows = arrived.reshape(experts * capacity, width)
    expert_sum = full_expert(own_rows, w_gate, w_up, w_down)
    finished = expert_sum.reshape(experts, capacity, width)
    returned = lax.all_to_all(finished, "dev", split_axis=0, concat_axis=0, tiled=True)
    flat_back = returned.reshape(experts * capacity, width)
    picked = flat_back[destination].reshape(tok_count, topk_count, width).astype(jnp.float32)
    moe_out = jnp.sum(picked * gate_weights[:, :, None], axis=1).astype(jnp.bfloat16)
    attended = jax.vmap(attend_row)(q_latent, q_rope, latent_cache, rope_cache, lengths)
    return (moe_out, attended)


def solution(mesh):
    placed = (
        P(("role", "dev"), None),
        P(("role", "dev"), None),
        P(("role", "dev"), None),
        P("dev", None, "role"),
        P("dev", None, "role"),
        P("dev", None, "role"),
        P(("role", "dev"), None, None),
        P(("role", "dev"), None),
        P(("role", "dev"), None, None),
        P(("role", "dev"), None, None),
        P(("role", "dev")),
    )
    return jax.shard_map(
        per_device,
        mesh=mesh,
        in_specs=placed,
        out_specs=(P(("role", "dev"), None), P(("role", "dev"), None, None)),
        check_vma=False,
    )
```

```python
import jax
import jax.numpy as jnp
from jax import lax
from jax.sharding import PartitionSpec as P
from jax.experimental import pallas as pl
from jax.experimental.pallas import tpu as pltpu
import functools

def gate_up_kernel(x_ref, g_ref, u_ref, h_ref):
    x = x_ref[...]
    gate_part = jnp.dot(x, g_ref[0], preferred_element_type=jnp.float32)
    up_part = jnp.dot(x, u_ref[0], preferred_element_type=jnp.float32)
    h_ref[...] = (jax.nn.silu(gate_part) * up_part).astype(h_ref.dtype)


def down_kernel(halves, h_ref, d_ref, o_ref):
    width = d_ref.shape[2]
    total = None
    for half in range(halves):
        term = lax.dot_general(
            h_ref[:, half * width:(half + 1) * width],
            d_ref[half],
            (((1,), (1,)), ((), ())),
            preferred_element_type=jnp.float32,
        )
        total = term if total is None else total + term
    o_ref[...] = total.astype(o_ref.dtype)


def expert_ffn(rows, gate_both, up_both, down_both, unit_tile=256, out_tile=512):
    count, width = rows.shape
    halves, _, units = gate_both.shape
    steps = units // unit_tile
    hidden = pl.pallas_call(
        gate_up_kernel,
        out_shape=jax.ShapeDtypeStruct((count, halves * units), jnp.bfloat16),
        grid=(halves, steps),
        in_specs=[
            pl.BlockSpec((count, width), lambda c, j: (0, 0)),
            pl.BlockSpec((1, width, unit_tile), lambda c, j: (c, 0, j)),
            pl.BlockSpec((1, width, unit_tile), lambda c, j: (c, 0, j)),
        ],
        out_specs=pl.BlockSpec((count, unit_tile), lambda c, j: (0, c * steps + j)),
        compiler_params=pltpu.CompilerParams(vmem_limit_bytes=48 * 1024 * 1024),
        cost_estimate=pl.CostEstimate(
            flops=4 * count * width * halves * units,
            transcendentals=count * halves * units,
            bytes_accessed=2 * (count * width + 2 * width * halves * units + count * halves * units),
        ),
    )(rows, gate_both, up_both)
    out_steps = width // out_tile
    return pl.pallas_call(
        functools.partial(down_kernel, halves),
        out_shape=jax.ShapeDtypeStruct((count, width), jnp.bfloat16),
        grid=(out_steps,),
        in_specs=[
            pl.BlockSpec((count, halves * units), lambda j: (0, 0)),
            pl.BlockSpec((halves, out_tile, units), lambda j: (0, j, 0)),
        ],
        out_specs=pl.BlockSpec((count, out_tile), lambda j: (0, j)),
        compiler_params=pltpu.CompilerParams(vmem_limit_bytes=48 * 1024 * 1024),
        cost_estimate=pl.CostEstimate(
            flops=2 * count * width * halves * units,
            transcendentals=0,
            bytes_accessed=2 * (count * width + width * halves * units + count * halves * units),
        ),
    )(hidden, down_both)


score_scale = 192.0 ** (-0.5)


def expert_block(chosen, gate_matrix, up_matrix, down_matrix):
    gate_part = jnp.dot(chosen, gate_matrix, preferred_element_type=jnp.float32)
    up_part = jnp.dot(chosen, up_matrix, preferred_element_type=jnp.float32)
    hidden_units = (jax.nn.silu(gate_part) * up_part).astype(jnp.bfloat16)
    return lax.dot_general(
        hidden_units, down_matrix, (((1,), (1,)), ((), ())), preferred_element_type=jnp.float32
    )


def full_expert(rows, w_gate, w_up, w_down):
    gate_both = lax.all_gather(w_gate[0], "role", axis=0)
    up_both = lax.all_gather(w_up[0], "role", axis=0)
    down_both = lax.all_gather(w_down[0], "role", axis=0)
    return expert_ffn(rows, gate_both, up_both, down_both)


def attend_row(query_lat, query_rope, cache_lat, cache_rope, length):
    head_count = query_lat.shape[0]
    rope_width = cache_rope.shape[0]
    scores = lax.dot_general(
        query_lat, cache_lat, (((1,), (1,)), ((), ())), preferred_element_type=jnp.float32
    )
    scores = scores + jnp.dot(
        query_rope.reshape(head_count, rope_width), cache_rope, preferred_element_type=jnp.float32
    )
    scores = scores * score_scale
    positions = jnp.arange(cache_lat.shape[0], dtype=jnp.int32)
    valid = (positions < length)[None, :]
    scores = jnp.where(valid, scores, jnp.float32(-1e30))
    highest = jnp.max(scores, axis=1, keepdims=True)
    weights = jnp.where(valid, jnp.exp(scores - highest), jnp.float32(0.0))
    probs = (weights / jnp.sum(weights, axis=1, keepdims=True)).astype(jnp.bfloat16)
    return jnp.dot(probs, cache_lat, preferred_element_type=jnp.float32).astype(jnp.bfloat16)


def per_device(
    moe_rows,
    expert_ids,
    gate_weights,
    w_gate,
    w_up,
    w_down,
    q_latent,
    q_rope,
    latent_cache,
    rope_cache,
    lengths,
):
    tok_count = moe_rows.shape[0]
    width = moe_rows.shape[1]
    topk_count = expert_ids.shape[1]
    experts = lax.axis_size("dev")
    capacity = min(tok_count, 2 * tok_count * topk_count // experts)
    flat_ids = expert_ids.reshape(-1)
    pair_count = flat_ids.shape[0]
    slot_count = experts * capacity
    one_hot = flat_ids[:, None] == jnp.arange(experts, dtype=jnp.int32)[None, :]
    pair_iota = jnp.arange(pair_count, dtype=jnp.int32)
    lower = (pair_iota[:, None] > pair_iota[None, :]).astype(jnp.bfloat16)
    earlier = jnp.dot(lower, one_hot.astype(jnp.bfloat16), preferred_element_type=jnp.float32)
    slot_index = jnp.sum(jnp.where(one_hot, earlier, 0.0), axis=1).astype(jnp.int32)
    destination = flat_ids * capacity + slot_index
    slot_iota = jnp.arange(slot_count, dtype=jnp.int32)
    picks = destination[:, None] == slot_iota[None, :]
    dispatch = jnp.any(picks.reshape(tok_count, topk_count, slot_count), axis=1)
    outgoing = lax.dot_general(
        dispatch.astype(jnp.bfloat16), moe_rows, (((0,), (0,)), ((), ())),
        preferred_element_type=jnp.float32,
    ).astype(jnp.bfloat16).reshape(experts, capacity, width)
    arrived = lax.all_to_all(outgoing, "dev", split_axis=0, concat_axis=0, tiled=True)
    own_rows = arrived.reshape(experts * capacity, width)
    expert_sum = full_expert(own_rows, w_gate, w_up, w_down)
    finished = expert_sum.reshape(experts, capacity, width)
    returned = lax.all_to_all(finished, "dev", split_axis=0, concat_axis=0, tiled=True)
    flat_back = returned.reshape(slot_count, width)
    picked = jnp.dot(
        picks.astype(jnp.bfloat16), flat_back, preferred_element_type=jnp.float32
    ).reshape(tok_count, topk_count, width)
    moe_out = jnp.sum(picked * gate_weights[:, :, None], axis=1).astype(jnp.bfloat16)
    attended = jax.vmap(attend_row)(q_latent, q_rope, latent_cache, rope_cache, lengths)
    return (moe_out, attended)


def solution(mesh):
    placed = (
        P(("role", "dev"), None),
        P(("role", "dev"), None),
        P(("role", "dev"), None),
        P("dev", None, "role"),
        P("dev", None, "role"),
        P("dev", None, "role"),
        P(("role", "dev"), None, None),
        P(("role", "dev"), None),
        P(("role", "dev"), None, None),
        P(("role", "dev"), None, None),
        P(("role", "dev")),
    )
    return jax.shard_map(
        per_device,
        mesh=mesh,
        in_specs=placed,
        out_specs=(P(("role", "dev"), None), P(("role", "dev"), None, None)),
        check_vma=False,
    )
```

```python
import jax
import jax.numpy as jnp
from jax import lax
from jax.sharding import PartitionSpec as P
from jax.experimental import pallas as pl
from jax.experimental.pallas import tpu as pltpu
import functools

def gate_up_kernel(x_ref, g_ref, u_ref, h_ref):
    x = x_ref[...]
    gate_part = jnp.dot(x, g_ref[...], preferred_element_type=jnp.float32)
    up_part = jnp.dot(x, u_ref[...], preferred_element_type=jnp.float32)
    h_ref[...] = (jax.nn.silu(gate_part) * up_part).astype(h_ref.dtype)


def down_kernel(h0_ref, h1_ref, d0_ref, d1_ref, o_ref):
    total = None
    for h_ref, d_ref in ((h0_ref, d0_ref), (h1_ref, d1_ref)):
        term = lax.dot_general(
            h_ref[...], d_ref[...], (((1,), (1,)), ((), ())), preferred_element_type=jnp.float32
        )
        total = term if total is None else total + term
    o_ref[...] = total.astype(o_ref.dtype)


def gate_up(rows, gate_matrix, up_matrix, unit_tile=256):
    count, width = rows.shape
    units = gate_matrix.shape[1]
    return pl.pallas_call(
        gate_up_kernel,
        out_shape=jax.ShapeDtypeStruct((count, units), jnp.bfloat16),
        grid=(units // unit_tile,),
        in_specs=[
            pl.BlockSpec((count, width), lambda j: (0, 0)),
            pl.BlockSpec((width, unit_tile), lambda j: (0, j)),
            pl.BlockSpec((width, unit_tile), lambda j: (0, j)),
        ],
        out_specs=pl.BlockSpec((count, unit_tile), lambda j: (0, j)),
        compiler_params=pltpu.CompilerParams(vmem_limit_bytes=48 * 1024 * 1024),
        cost_estimate=pl.CostEstimate(
            flops=4 * count * width * units,
            transcendentals=count * units,
            bytes_accessed=2 * (count * width + 2 * width * units + count * units),
        ),
    )(rows, gate_matrix, up_matrix)


def down(h0, h1, d0, d1, out_tile=512):
    count, units = h0.shape
    width = d0.shape[0]
    return pl.pallas_call(
        down_kernel,
        out_shape=jax.ShapeDtypeStruct((count, width), jnp.bfloat16),
        grid=(width // out_tile,),
        in_specs=[
            pl.BlockSpec((count, units), lambda j: (0, 0)),
            pl.BlockSpec((count, units), lambda j: (0, 0)),
            pl.BlockSpec((out_tile, units), lambda j: (j, 0)),
            pl.BlockSpec((out_tile, units), lambda j: (j, 0)),
        ],
        out_specs=pl.BlockSpec((count, out_tile), lambda j: (0, j)),
        compiler_params=pltpu.CompilerParams(vmem_limit_bytes=48 * 1024 * 1024),
        cost_estimate=pl.CostEstimate(
            flops=4 * count * width * units,
            transcendentals=0,
            bytes_accessed=2 * (count * width + 2 * width * units + 2 * count * units),
        ),
    )(h0, h1, d0, d1)


def other_half(w):
    return lax.ppermute(w, "role", [(0, 1), (1, 0)])


def full_expert(rows, w_gate, w_up, w_down):
    gate_own, up_own, down_own = w_gate[0], w_up[0], w_down[0]
    gate_other, up_other, down_other = other_half(gate_own), other_half(up_own), other_half(down_own)
    h0 = gate_up(rows, gate_own, up_own)
    h1 = gate_up(rows, gate_other, up_other)
    return down(h0, h1, down_own, down_other)


score_scale = 192.0 ** (-0.5)


def attend_row(query_lat, query_rope, cache_lat, cache_rope, length):
    head_count = query_lat.shape[0]
    rope_width = cache_rope.shape[0]
    scores = lax.dot_general(
        query_lat, cache_lat, (((1,), (1,)), ((), ())), preferred_element_type=jnp.float32
    )
    scores = scores + jnp.dot(
        query_rope.reshape(head_count, rope_width), cache_rope, preferred_element_type=jnp.float32
    )
    scores = scores * score_scale
    positions = jnp.arange(cache_lat.shape[0], dtype=jnp.int32)
    valid = (positions < length)[None, :]
    scores = jnp.where(valid, scores, jnp.float32(-1e30))
    highest = jnp.max(scores, axis=1, keepdims=True)
    weights = jnp.where(valid, jnp.exp(scores - highest), jnp.float32(0.0))
    probs = (weights / jnp.sum(weights, axis=1, keepdims=True)).astype(jnp.bfloat16)
    return jnp.dot(probs, cache_lat, preferred_element_type=jnp.float32).astype(jnp.bfloat16)


def per_device(
    moe_rows,
    expert_ids,
    gate_weights,
    w_gate,
    w_up,
    w_down,
    q_latent,
    q_rope,
    latent_cache,
    rope_cache,
    lengths,
):
    tok_count = moe_rows.shape[0]
    width = moe_rows.shape[1]
    topk_count = expert_ids.shape[1]
    experts = lax.axis_size("dev")
    capacity = min(tok_count, 2 * tok_count * topk_count // experts)
    flat_ids = expert_ids.reshape(-1)
    pair_count = flat_ids.shape[0]
    slot_count = experts * capacity
    one_hot = flat_ids[:, None] == jnp.arange(experts, dtype=jnp.int32)[None, :]
    pair_iota = jnp.arange(pair_count, dtype=jnp.int32)
    lower = (pair_iota[:, None] > pair_iota[None, :]).astype(jnp.bfloat16)
    earlier = jnp.dot(lower, one_hot.astype(jnp.bfloat16), preferred_element_type=jnp.float32)
    slot_index = jnp.sum(jnp.where(one_hot, earlier, 0.0), axis=1).astype(jnp.int32)
    destination = flat_ids * capacity + slot_index
    slot_iota = jnp.arange(slot_count, dtype=jnp.int32)
    picks = destination[:, None] == slot_iota[None, :]
    dispatch = jnp.any(picks.reshape(tok_count, topk_count, slot_count), axis=1)
    outgoing = lax.dot_general(
        dispatch.astype(jnp.bfloat16), moe_rows, (((0,), (0,)), ((), ())),
        preferred_element_type=jnp.float32,
    ).astype(jnp.bfloat16).reshape(experts, capacity, width)
    arrived = lax.all_to_all(outgoing, "dev", split_axis=0, concat_axis=0, tiled=True)
    own_rows = arrived.reshape(experts * capacity, width)
    expert_sum = full_expert(own_rows, w_gate, w_up, w_down)
    finished = expert_sum.reshape(experts, capacity, width)
    returned = lax.all_to_all(finished, "dev", split_axis=0, concat_axis=0, tiled=True)
    flat_back = returned.reshape(slot_count, width)
    picked = jnp.dot(
        picks.astype(jnp.bfloat16), flat_back, preferred_element_type=jnp.float32
    ).reshape(tok_count, topk_count, width)
    moe_out = jnp.sum(picked * gate_weights[:, :, None], axis=1).astype(jnp.bfloat16)
    attended = jax.vmap(attend_row)(q_latent, q_rope, latent_cache, rope_cache, lengths)
    return (moe_out, attended)


def solution(mesh):
    placed = (
        P(("role", "dev"), None),
        P(("role", "dev"), None),
        P(("role", "dev"), None),
        P("dev", None, "role"),
        P("dev", None, "role"),
        P("dev", None, "role"),
        P(("role", "dev"), None, None),
        P(("role", "dev"), None),
        P(("role", "dev"), None, None),
        P(("role", "dev"), None, None),
        P(("role", "dev")),
    )
    return jax.shard_map(
        per_device,
        mesh=mesh,
        in_specs=placed,
        out_specs=(P(("role", "dev"), None), P(("role", "dev"), None, None)),
        check_vma=False,
    )
```

```python
import jax
import jax.numpy as jnp
from jax import lax
from jax.sharding import PartitionSpec as P
from jax.experimental import pallas as pl
from jax.experimental.pallas import tpu as pltpu
import functools

def gate_up_kernel(x_ref, g_ref, u_ref, h_ref):
    x = x_ref[...]
    gate_part = jnp.dot(x, g_ref[...], preferred_element_type=jnp.float32)
    up_part = jnp.dot(x, u_ref[...], preferred_element_type=jnp.float32)
    h_ref[...] = (jax.nn.silu(gate_part) * up_part).astype(h_ref.dtype)


def down_kernel(h0_ref, h1_ref, d0_ref, d1_ref, o_ref):
    total = None
    for h_ref, d_ref in ((h0_ref, d0_ref), (h1_ref, d1_ref)):
        term = lax.dot_general(
            h_ref[...], d_ref[...], (((1,), (1,)), ((), ())), preferred_element_type=jnp.float32
        )
        total = term if total is None else total + term
    o_ref[...] = total.astype(o_ref.dtype)


def gate_up(rows, gate_matrix, up_matrix, unit_tile=256):
    count, width = rows.shape
    units = gate_matrix.shape[1]
    return pl.pallas_call(
        gate_up_kernel,
        out_shape=jax.ShapeDtypeStruct((count, units), jnp.bfloat16),
        grid=(units // unit_tile,),
        in_specs=[
            pl.BlockSpec((count, width), lambda j: (0, 0)),
            pl.BlockSpec((width, unit_tile), lambda j: (0, j)),
            pl.BlockSpec((width, unit_tile), lambda j: (0, j)),
        ],
        out_specs=pl.BlockSpec((count, unit_tile), lambda j: (0, j)),
        compiler_params=pltpu.CompilerParams(vmem_limit_bytes=48 * 1024 * 1024),
        cost_estimate=pl.CostEstimate(
            flops=4 * count * width * units,
            transcendentals=count * units,
            bytes_accessed=2 * (count * width + 2 * width * units + count * units),
        ),
    )(rows, gate_matrix, up_matrix)


def down(h0, h1, d0, d1, out_tile=512):
    count, units = h0.shape
    width = d0.shape[0]
    return pl.pallas_call(
        down_kernel,
        out_shape=jax.ShapeDtypeStruct((count, width), jnp.bfloat16),
        grid=(width // out_tile,),
        in_specs=[
            pl.BlockSpec((count, units), lambda j: (0, 0)),
            pl.BlockSpec((count, units), lambda j: (0, 0)),
            pl.BlockSpec((out_tile, units), lambda j: (j, 0)),
            pl.BlockSpec((out_tile, units), lambda j: (j, 0)),
        ],
        out_specs=pl.BlockSpec((count, out_tile), lambda j: (0, j)),
        compiler_params=pltpu.CompilerParams(vmem_limit_bytes=48 * 1024 * 1024),
        cost_estimate=pl.CostEstimate(
            flops=4 * count * width * units,
            transcendentals=0,
            bytes_accessed=2 * (count * width + 2 * width * units + 2 * count * units),
        ),
    )(h0, h1, d0, d1)


def other_half(w):
    return lax.ppermute(w, "role", [(0, 1), (1, 0)])


def full_expert(rows, own, other):
    h0 = gate_up(rows, own[0], own[1])
    h1 = gate_up(rows, other[0], other[1])
    return down(h0, h1, own[2], other[2])


score_scale = 192.0 ** (-0.5)


def attend_row(query_lat, query_rope, cache_lat, cache_rope, length):
    head_count = query_lat.shape[0]
    rope_width = cache_rope.shape[0]
    scores = lax.dot_general(
        query_lat, cache_lat, (((1,), (1,)), ((), ())), preferred_element_type=jnp.float32
    )
    scores = scores + jnp.dot(
        query_rope.reshape(head_count, rope_width), cache_rope, preferred_element_type=jnp.float32
    )
    scores = scores * score_scale
    positions = jnp.arange(cache_lat.shape[0], dtype=jnp.int32)
    valid = (positions < length)[None, :]
    scores = jnp.where(valid, scores, jnp.float32(-1e30))
    highest = jnp.max(scores, axis=1, keepdims=True)
    weights = jnp.where(valid, jnp.exp(scores - highest), jnp.float32(0.0))
    probs = (weights / jnp.sum(weights, axis=1, keepdims=True)).astype(jnp.bfloat16)
    return jnp.dot(probs, cache_lat, preferred_element_type=jnp.float32).astype(jnp.bfloat16)


def per_device(
    moe_rows,
    expert_ids,
    gate_weights,
    w_gate,
    w_up,
    w_down,
    q_latent,
    q_rope,
    latent_cache,
    rope_cache,
    lengths,
):
    tok_count = moe_rows.shape[0]
    width = moe_rows.shape[1]
    topk_count = expert_ids.shape[1]
    experts = lax.axis_size("dev")
    capacity = min(tok_count, 2 * tok_count * topk_count // experts)
    flat_ids = expert_ids.reshape(-1)
    pair_count = flat_ids.shape[0]
    slot_count = experts * capacity
    one_hot = flat_ids[:, None] == jnp.arange(experts, dtype=jnp.int32)[None, :]
    pair_iota = jnp.arange(pair_count, dtype=jnp.int32)
    lower = (pair_iota[:, None] > pair_iota[None, :]).astype(jnp.bfloat16)
    earlier = jnp.dot(lower, one_hot.astype(jnp.bfloat16), preferred_element_type=jnp.float32)
    slot_index = jnp.sum(jnp.where(one_hot, earlier, 0.0), axis=1).astype(jnp.int32)
    destination = flat_ids * capacity + slot_index
    slot_iota = jnp.arange(slot_count, dtype=jnp.int32)
    picks = destination[:, None] == slot_iota[None, :]
    dispatch = jnp.any(picks.reshape(tok_count, topk_count, slot_count), axis=1)
    dispatch = dispatch.astype(jnp.bfloat16).reshape(tok_count, experts, capacity)
    pick_matrix = picks.astype(jnp.bfloat16).reshape(pair_count, experts, capacity)
    own = (w_gate[0], w_up[0], w_down[0])
    other = tuple(other_half(w) for w in own)
    chunks = 2
    per = capacity // chunks
    picked = None
    for chunk in range(chunks):
        lo, hi = chunk * per, (chunk + 1) * per
        outgoing = lax.dot_general(
            dispatch[:, :, lo:hi].reshape(tok_count, experts * per), moe_rows,
            (((0,), (0,)), ((), ())), preferred_element_type=jnp.float32,
        ).astype(jnp.bfloat16).reshape(experts, per, width)
        arrived = lax.all_to_all(outgoing, "dev", split_axis=0, concat_axis=0, tiled=True)
        finished = full_expert(arrived.reshape(experts * per, width), own, other)
        returned = lax.all_to_all(
            finished.reshape(experts, per, width), "dev", split_axis=0, concat_axis=0, tiled=True
        )
        term = jnp.dot(
            pick_matrix[:, :, lo:hi].reshape(pair_count, experts * per),
            returned.reshape(experts * per, width),
            preferred_element_type=jnp.float32,
        )
        picked = term if picked is None else picked + term
    picked = picked.reshape(tok_count, topk_count, width)
    moe_out = jnp.sum(picked * gate_weights[:, :, None], axis=1).astype(jnp.bfloat16)
    attended = jax.vmap(attend_row)(q_latent, q_rope, latent_cache, rope_cache, lengths)
    return (moe_out, attended)


def solution(mesh):
    placed = (
        P(("role", "dev"), None),
        P(("role", "dev"), None),
        P(("role", "dev"), None),
        P("dev", None, "role"),
        P("dev", None, "role"),
        P("dev", None, "role"),
        P(("role", "dev"), None, None),
        P(("role", "dev"), None),
        P(("role", "dev"), None, None),
        P(("role", "dev"), None, None),
        P(("role", "dev")),
    )
    return jax.shard_map(
        per_device,
        mesh=mesh,
        in_specs=placed,
        out_specs=(P(("role", "dev"), None), P(("role", "dev"), None, None)),
        check_vma=False,
    )
```

```python
import jax
import jax.numpy as jnp
from jax import lax
from jax.sharding import PartitionSpec as P
from jax.experimental import pallas as pl
from jax.experimental.pallas import tpu as pltpu
import functools

def partial_kernel(x_ref, g_ref, u_ref, pg_ref, pu_ref):
    x = x_ref[...]
    pg_ref[...] = jnp.dot(x, g_ref[...], preferred_element_type=jnp.float32)
    pu_ref[...] = jnp.dot(x, u_ref[...], preferred_element_type=jnp.float32)


def finish_kernel(x_ref, g_ref, u_ref, pg_ref, pu_ref, h_ref):
    x = x_ref[...]
    gate_part = pg_ref[...] + jnp.dot(x, g_ref[...], preferred_element_type=jnp.float32)
    up_part = pu_ref[...] + jnp.dot(x, u_ref[...], preferred_element_type=jnp.float32)
    h_ref[...] = (jax.nn.silu(gate_part) * up_part).astype(h_ref.dtype)


def down_kernel(h0_ref, h1_ref, d0_ref, d1_ref, o_ref):
    total = None
    for h_ref, d_ref in ((h0_ref, d0_ref), (h1_ref, d1_ref)):
        term = lax.dot_general(
            h_ref[...], d_ref[...], (((1,), (1,)), ((), ())), preferred_element_type=jnp.float32
        )
        total = term if total is None else total + term
    o_ref[...] = total.astype(o_ref.dtype)


def gate_up_partial(rows, gate_matrix, up_matrix, unit_tile=256):
    count, depth = rows.shape
    units = gate_matrix.shape[1]
    part = jax.ShapeDtypeStruct((count, units), jnp.float32)
    return pl.pallas_call(
        partial_kernel,
        out_shape=(part, part),
        grid=(units // unit_tile,),
        in_specs=[
            pl.BlockSpec((count, depth), lambda j: (0, 0)),
            pl.BlockSpec((depth, unit_tile), lambda j: (0, j)),
            pl.BlockSpec((depth, unit_tile), lambda j: (0, j)),
        ],
        out_specs=[pl.BlockSpec((count, unit_tile), lambda j: (0, j))] * 2,
        compiler_params=pltpu.CompilerParams(vmem_limit_bytes=48 * 1024 * 1024),
        cost_estimate=pl.CostEstimate(
            flops=4 * count * depth * units,
            transcendentals=0,
            bytes_accessed=2 * (count * depth + 2 * depth * units) + 8 * count * units,
        ),
    )(rows, gate_matrix, up_matrix)


def gate_up_finish(rows, gate_matrix, up_matrix, partials, unit_tile=256):
    count, depth = rows.shape
    units = gate_matrix.shape[1]
    tile = pl.BlockSpec((count, unit_tile), lambda j: (0, j))
    return pl.pallas_call(
        finish_kernel,
        out_shape=jax.ShapeDtypeStruct((count, units), jnp.bfloat16),
        grid=(units // unit_tile,),
        in_specs=[
            pl.BlockSpec((count, depth), lambda j: (0, 0)),
            pl.BlockSpec((depth, unit_tile), lambda j: (1, j)),
            pl.BlockSpec((depth, unit_tile), lambda j: (1, j)),
            tile,
            tile,
        ],
        out_specs=tile,
        compiler_params=pltpu.CompilerParams(vmem_limit_bytes=48 * 1024 * 1024),
        cost_estimate=pl.CostEstimate(
            flops=4 * count * depth * units,
            transcendentals=count * units,
            bytes_accessed=2 * (count * depth + 2 * depth * units + count * units) + 8 * count * units,
        ),
    )(rows, gate_matrix, up_matrix, *partials)


def down_columns(h0, h1, d0, d1, first, count_out, out_tile=256):
    count, units = h0.shape
    offset = first // out_tile
    return pl.pallas_call(
        down_kernel,
        out_shape=jax.ShapeDtypeStruct((count, count_out), jnp.bfloat16),
        grid=(count_out // out_tile,),
        in_specs=[
            pl.BlockSpec((count, units), lambda j: (0, 0)),
            pl.BlockSpec((count, units), lambda j: (0, 0)),
            pl.BlockSpec((out_tile, units), lambda j: (j + offset, 0)),
            pl.BlockSpec((out_tile, units), lambda j: (j + offset, 0)),
        ],
        out_specs=pl.BlockSpec((count, out_tile), lambda j: (0, j)),
        compiler_params=pltpu.CompilerParams(vmem_limit_bytes=48 * 1024 * 1024),
        cost_estimate=pl.CostEstimate(
            flops=4 * count * count_out * units,
            transcendentals=0,
            bytes_accessed=2 * (count * count_out + 2 * count_out * units + 2 * count * units),
        ),
    )(h0, h1, d0, d1)


def other_half(w):
    return lax.ppermute(w, "role", [(0, 1), (1, 0)])


score_scale = 192.0 ** (-0.5)


def attend_row(query_lat, query_rope, cache_lat, cache_rope, length):
    head_count = query_lat.shape[0]
    rope_width = cache_rope.shape[0]
    scores = lax.dot_general(
        query_lat, cache_lat, (((1,), (1,)), ((), ())), preferred_element_type=jnp.float32
    )
    scores = scores + jnp.dot(
        query_rope.reshape(head_count, rope_width), cache_rope, preferred_element_type=jnp.float32
    )
    scores = scores * score_scale
    positions = jnp.arange(cache_lat.shape[0], dtype=jnp.int32)
    valid = (positions < length)[None, :]
    scores = jnp.where(valid, scores, jnp.float32(-1e30))
    highest = jnp.max(scores, axis=1, keepdims=True)
    weights = jnp.where(valid, jnp.exp(scores - highest), jnp.float32(0.0))
    probs = (weights / jnp.sum(weights, axis=1, keepdims=True)).astype(jnp.bfloat16)
    return jnp.dot(probs, cache_lat, preferred_element_type=jnp.float32).astype(jnp.bfloat16)


def per_device(
    moe_rows,
    expert_ids,
    gate_weights,
    w_gate,
    w_up,
    w_down,
    q_latent,
    q_rope,
    latent_cache,
    rope_cache,
    lengths,
):
    tok_count = moe_rows.shape[0]
    width = moe_rows.shape[1]
    topk_count = expert_ids.shape[1]
    experts = lax.axis_size("dev")
    capacity = min(tok_count, 2 * tok_count * topk_count // experts)
    flat_ids = expert_ids.reshape(-1)
    pair_count = flat_ids.shape[0]
    slot_count = experts * capacity
    one_hot = flat_ids[:, None] == jnp.arange(experts, dtype=jnp.int32)[None, :]
    pair_iota = jnp.arange(pair_count, dtype=jnp.int32)
    lower = (pair_iota[:, None] > pair_iota[None, :]).astype(jnp.bfloat16)
    earlier = jnp.dot(lower, one_hot.astype(jnp.bfloat16), preferred_element_type=jnp.float32)
    slot_index = jnp.sum(jnp.where(one_hot, earlier, 0.0), axis=1).astype(jnp.int32)
    destination = flat_ids * capacity + slot_index
    slot_iota = jnp.arange(slot_count, dtype=jnp.int32)
    picks = destination[:, None] == slot_iota[None, :]
    dispatch = jnp.any(picks.reshape(tok_count, topk_count, slot_count), axis=1).astype(jnp.bfloat16)
    half = width // 2
    arrived = []
    for lo in (0, half):
        outgoing = lax.dot_general(
            dispatch, moe_rows[:, lo:lo + half], (((0,), (0,)), ((), ())),
            preferred_element_type=jnp.float32,
        ).astype(jnp.bfloat16).reshape(experts, capacity, half)
        arrived.append(
            lax.all_to_all(outgoing, "dev", split_axis=0, concat_axis=0, tiled=True).reshape(slot_count, half)
        )
    own = (w_gate[0], w_up[0], w_down[0])
    other = tuple(other_half(w) for w in own)
    partials = [gate_up_partial(arrived[0], w[0], w[1]) for w in (own, other)]
    h0, h1 = [gate_up_finish(arrived[1], w[0], w[1], p) for w, p in zip((own, other), partials)]
    pick_matrix = picks.astype(jnp.bfloat16)
    picked = []
    for lo in (0, half):
        finished = down_columns(h0, h1, own[2], other[2], lo, half)
        returned = lax.all_to_all(
            finished.reshape(experts, capacity, half), "dev", split_axis=0, concat_axis=0, tiled=True
        )
        picked.append(jnp.dot(pick_matrix, returned.reshape(slot_count, half), preferred_element_type=jnp.float32))
    picked = jnp.concatenate(picked, axis=1).reshape(tok_count, topk_count, width)
    moe_out = jnp.sum(picked * gate_weights[:, :, None], axis=1).astype(jnp.bfloat16)
    attended = jax.vmap(attend_row)(q_latent, q_rope, latent_cache, rope_cache, lengths)
    return (moe_out, attended)


def solution(mesh):
    placed = (
        P(("role", "dev"), None),
        P(("role", "dev"), None),
        P(("role", "dev"), None),
        P("dev", None, "role"),
        P("dev", None, "role"),
        P("dev", None, "role"),
        P(("role", "dev"), None, None),
        P(("role", "dev"), None),
        P(("role", "dev"), None, None),
        P(("role", "dev"), None, None),
        P(("role", "dev")),
    )
    return jax.shard_map(
        per_device,
        mesh=mesh,
        in_specs=placed,
        out_specs=(P(("role", "dev"), None), P(("role", "dev"), None, None)),
        check_vma=False,
    )
```

```python
import jax
import jax.numpy as jnp
from jax import lax
from jax.sharding import PartitionSpec as P
from jax.experimental import pallas as pl
from jax.experimental.pallas import tpu as pltpu
import functools

def gate_up_kernel(x_ref, g_ref, u_ref, h_ref):
    x = x_ref[...]
    gate_part = jnp.dot(x, g_ref[...], preferred_element_type=jnp.float32)
    up_part = jnp.dot(x, u_ref[...], preferred_element_type=jnp.float32)
    h_ref[...] = (jax.nn.silu(gate_part) * up_part).astype(h_ref.dtype)


def down_kernel(h0_ref, h1_ref, d0_ref, d1_ref, o_ref):
    total = None
    for h_ref, d_ref in ((h0_ref, d0_ref), (h1_ref, d1_ref)):
        term = lax.dot_general(
            h_ref[...], d_ref[...], (((1,), (1,)), ((), ())), preferred_element_type=jnp.float32
        )
        total = term if total is None else total + term
    o_ref[...] = total.astype(o_ref.dtype)


def gate_up(rows, gate_matrix, up_matrix, unit_tile=256):
    count, width = rows.shape
    units = gate_matrix.shape[1]
    return pl.pallas_call(
        gate_up_kernel,
        out_shape=jax.ShapeDtypeStruct((count, units), jnp.bfloat16),
        grid=(units // unit_tile,),
        in_specs=[
            pl.BlockSpec((count, width), lambda j: (0, 0)),
            pl.BlockSpec((width, unit_tile), lambda j: (0, j)),
            pl.BlockSpec((width, unit_tile), lambda j: (0, j)),
        ],
        out_specs=pl.BlockSpec((count, unit_tile), lambda j: (0, j)),
        compiler_params=pltpu.CompilerParams(vmem_limit_bytes=48 * 1024 * 1024),
        cost_estimate=pl.CostEstimate(
            flops=4 * count * width * units,
            transcendentals=count * units,
            bytes_accessed=2 * (count * width + 2 * width * units + count * units),
        ),
    )(rows, gate_matrix, up_matrix)


def down(h0, h1, d0, d1, out_tile=512):
    count, units = h0.shape
    width = d0.shape[0]
    return pl.pallas_call(
        down_kernel,
        out_shape=jax.ShapeDtypeStruct((count, width), jnp.bfloat16),
        grid=(width // out_tile,),
        in_specs=[
            pl.BlockSpec((count, units), lambda j: (0, 0)),
            pl.BlockSpec((count, units), lambda j: (0, 0)),
            pl.BlockSpec((out_tile, units), lambda j: (j, 0)),
            pl.BlockSpec((out_tile, units), lambda j: (j, 0)),
        ],
        out_specs=pl.BlockSpec((count, out_tile), lambda j: (0, j)),
        compiler_params=pltpu.CompilerParams(vmem_limit_bytes=48 * 1024 * 1024),
        cost_estimate=pl.CostEstimate(
            flops=4 * count * width * units,
            transcendentals=0,
            bytes_accessed=2 * (count * width + 2 * width * units + 2 * count * units),
        ),
    )(h0, h1, d0, d1)


def other_half(w):
    return lax.ppermute(w, "role", [(0, 1), (1, 0)])


def full_expert(rows, w_gate, w_up, w_down):
    gate_own, up_own, down_own = w_gate[0], w_up[0], w_down[0]
    gate_other, up_other, down_other = other_half(gate_own), other_half(up_own), other_half(down_own)
    h0 = gate_up(rows, gate_own, up_own)
    h1 = gate_up(rows, gate_other, up_other)
    return down(h0, h1, down_own, down_other)


score_scale = 192.0 ** (-0.5)


def attend_row(query_lat, query_rope, cache_lat, cache_rope, length):
    head_count = query_lat.shape[0]
    rope_width = cache_rope.shape[0]
    scores = lax.dot_general(
        query_lat, cache_lat, (((1,), (1,)), ((), ())), preferred_element_type=jnp.float32
    )
    scores = scores + jnp.dot(
        query_rope.reshape(head_count, rope_width), cache_rope, preferred_element_type=jnp.float32
    )
    scores = scores * score_scale
    positions = jnp.arange(cache_lat.shape[0], dtype=jnp.int32)
    valid = (positions < length)[None, :]
    scores = jnp.where(valid, scores, jnp.float32(-1e30))
    highest = jnp.max(scores, axis=1, keepdims=True)
    weights = jnp.where(valid, jnp.exp(scores - highest), jnp.float32(0.0))
    probs = (weights / jnp.sum(weights, axis=1, keepdims=True)).astype(jnp.bfloat16)
    return jnp.dot(probs, cache_lat, preferred_element_type=jnp.float32).astype(jnp.bfloat16)


def per_device(
    moe_rows,
    expert_ids,
    gate_weights,
    w_gate,
    w_up,
    w_down,
    q_latent,
    q_rope,
    latent_cache,
    rope_cache,
    lengths,
):
    tok_count = moe_rows.shape[0]
    width = moe_rows.shape[1]
    topk_count = expert_ids.shape[1]
    experts = lax.axis_size("dev")
    capacity = min(tok_count, 2 * tok_count * topk_count // experts)
    flat_ids = expert_ids.reshape(-1)
    pair_count = flat_ids.shape[0]
    slot_count = experts * capacity
    one_hot = flat_ids[:, None] == jnp.arange(experts, dtype=jnp.int32)[None, :]
    pair_iota = jnp.arange(pair_count, dtype=jnp.int32)
    lower = (pair_iota[:, None] > pair_iota[None, :]).astype(jnp.bfloat16)
    earlier = jnp.dot(lower, one_hot.astype(jnp.bfloat16), preferred_element_type=jnp.float32)
    slot_index = jnp.sum(jnp.where(one_hot, earlier, 0.0), axis=1).astype(jnp.int32)
    destination = flat_ids * capacity + slot_index
    slot_iota = jnp.arange(slot_count, dtype=jnp.int32)
    picks = destination[:, None] == slot_iota[None, :]
    dispatch = jnp.any(
        destination.reshape(tok_count, topk_count)[None, :, :] == slot_iota[:, None, None], axis=2
    )
    outgoing = jnp.dot(
        dispatch.astype(jnp.bfloat16), moe_rows, preferred_element_type=jnp.float32
    ).astype(jnp.bfloat16).reshape(experts, capacity, width)
    arrived = lax.all_to_all(outgoing, "dev", split_axis=0, concat_axis=0, tiled=True)
    own_rows = arrived.reshape(experts * capacity, width)
    expert_sum = full_expert(own_rows, w_gate, w_up, w_down)
    finished = expert_sum.reshape(experts, capacity, width)
    returned = lax.all_to_all(finished, "dev", split_axis=0, concat_axis=0, tiled=True)
    flat_back = returned.reshape(slot_count, width)
    weighted = jnp.sum(
        jnp.where(picks, gate_weights.reshape(pair_count)[:, None], 0.0).reshape(tok_count, topk_count, slot_count),
        axis=1,
    )
    moe_out = jnp.dot(
        weighted, flat_back.astype(jnp.float32), precision=lax.Precision.HIGHEST,
        preferred_element_type=jnp.float32,
    ).astype(jnp.bfloat16)
    attended = jax.vmap(attend_row)(q_latent, q_rope, latent_cache, rope_cache, lengths)
    return (moe_out, attended)


def solution(mesh):
    placed = (
        P(("role", "dev"), None),
        P(("role", "dev"), None),
        P(("role", "dev"), None),
        P("dev", None, "role"),
        P("dev", None, "role"),
        P("dev", None, "role"),
        P(("role", "dev"), None, None),
        P(("role", "dev"), None),
        P(("role", "dev"), None, None),
        P(("role", "dev"), None, None),
        P(("role", "dev")),
    )
    return jax.shard_map(
        per_device,
        mesh=mesh,
        in_specs=placed,
        out_specs=(P(("role", "dev"), None), P(("role", "dev"), None, None)),
        check_vma=False,
    )
```

```python
import jax
import jax.numpy as jnp
from jax import lax
from jax.sharding import PartitionSpec as P
from jax.experimental import pallas as pl
from jax.experimental.pallas import tpu as pltpu
import functools

def gate_up_kernel(x_ref, g_ref, u_ref, h_ref):
    x = x_ref[...]
    gate_part = jnp.dot(x, g_ref[...], preferred_element_type=jnp.float32)
    up_part = jnp.dot(x, u_ref[...], preferred_element_type=jnp.float32)
    h_ref[...] = (jax.nn.silu(gate_part) * up_part).astype(h_ref.dtype)


def down_kernel(h0_ref, h1_ref, d0_ref, d1_ref, o_ref):
    total = None
    for h_ref, d_ref in ((h0_ref, d0_ref), (h1_ref, d1_ref)):
        term = lax.dot_general(
            h_ref[...], d_ref[...], (((1,), (1,)), ((), ())), preferred_element_type=jnp.float32
        )
        total = term if total is None else total + term
    o_ref[...] = total.astype(o_ref.dtype)


def gate_up(rows, gate_matrix, up_matrix, unit_tile=256):
    count, width = rows.shape
    units = gate_matrix.shape[1]
    return pl.pallas_call(
        gate_up_kernel,
        out_shape=jax.ShapeDtypeStruct((count, units), jnp.bfloat16),
        grid=(units // unit_tile,),
        in_specs=[
            pl.BlockSpec((count, width), lambda j: (0, 0)),
            pl.BlockSpec((width, unit_tile), lambda j: (0, j)),
            pl.BlockSpec((width, unit_tile), lambda j: (0, j)),
        ],
        out_specs=pl.BlockSpec((count, unit_tile), lambda j: (0, j)),
        compiler_params=pltpu.CompilerParams(vmem_limit_bytes=48 * 1024 * 1024),
        cost_estimate=pl.CostEstimate(
            flops=4 * count * width * units,
            transcendentals=count * units,
            bytes_accessed=2 * (count * width + 2 * width * units + count * units),
        ),
    )(rows, gate_matrix, up_matrix)


def down(h0, h1, d0, d1, out_tile=512):
    count, units = h0.shape
    width = d0.shape[0]
    return pl.pallas_call(
        down_kernel,
        out_shape=jax.ShapeDtypeStruct((count, width), jnp.bfloat16),
        grid=(width // out_tile,),
        in_specs=[
            pl.BlockSpec((count, units), lambda j: (0, 0)),
            pl.BlockSpec((count, units), lambda j: (0, 0)),
            pl.BlockSpec((out_tile, units), lambda j: (j, 0)),
            pl.BlockSpec((out_tile, units), lambda j: (j, 0)),
        ],
        out_specs=pl.BlockSpec((count, out_tile), lambda j: (0, j)),
        compiler_params=pltpu.CompilerParams(vmem_limit_bytes=48 * 1024 * 1024),
        cost_estimate=pl.CostEstimate(
            flops=4 * count * width * units,
            transcendentals=0,
            bytes_accessed=2 * (count * width + 2 * width * units + 2 * count * units),
        ),
    )(h0, h1, d0, d1)


def other_half(w):
    return lax.ppermute(w, "role", [(0, 1), (1, 0)])


def ffn_kernel(steps, x_ref, go_ref, uo_ref, gt_ref, ut_ref, do_ref, dt_ref, o_ref, h_ref):
    i = pl.program_id(0)
    tile = go_ref.shape[1]
    units = h_ref.shape[1] // 2

    def hidden(g_ref, u_ref, column):
        x = x_ref[...]
        gate_part = jnp.dot(x, g_ref[...], preferred_element_type=jnp.float32)
        up_part = jnp.dot(x, u_ref[...], preferred_element_type=jnp.float32)
        h_ref[:, pl.ds(pl.multiple_of(column, tile), tile)] = (
            jax.nn.silu(gate_part) * up_part
        ).astype(h_ref.dtype)

    @pl.when(i < steps)
    def _():
        hidden(go_ref, uo_ref, i * tile)

    @pl.when((i >= steps) & (i < 2 * steps))
    def _():
        hidden(gt_ref, ut_ref, units + (i - steps) * tile)

    @pl.when(i >= 2 * steps)
    def _():
        total = lax.dot_general(
            h_ref[:, :units], do_ref[...], (((1,), (1,)), ((), ())), preferred_element_type=jnp.float32
        )
        total = total + lax.dot_general(
            h_ref[:, units:], dt_ref[...], (((1,), (1,)), ((), ())), preferred_element_type=jnp.float32
        )
        o_ref[...] = total.astype(o_ref.dtype)


def full_expert(rows, w_gate, w_up, w_down, unit_tile=256, out_tile=896):
    count, width = rows.shape
    own = (w_gate[0], w_up[0], w_down[0])
    other = tuple(other_half(w) for w in own)
    units = own[0].shape[1]
    steps = units // unit_tile
    outs = width // out_tile

    def own_map(i):
        return (0, jnp.minimum(i, steps - 1))

    def other_map(i):
        return (0, jnp.clip(i - steps, 0, steps - 1))

    def down_map(i):
        return (jnp.clip(i - 2 * steps, 0, outs - 1), 0)

    unit_block = (width, unit_tile)
    return pl.pallas_call(
        functools.partial(ffn_kernel, steps),
        out_shape=jax.ShapeDtypeStruct((count, width), jnp.bfloat16),
        grid=(2 * steps + outs,),
        in_specs=[
            pl.BlockSpec((count, width), lambda i: (0, 0)),
            pl.BlockSpec(unit_block, own_map),
            pl.BlockSpec(unit_block, own_map),
            pl.BlockSpec(unit_block, other_map),
            pl.BlockSpec(unit_block, other_map),
            pl.BlockSpec((out_tile, units), down_map),
            pl.BlockSpec((out_tile, units), down_map),
        ],
        out_specs=pl.BlockSpec((count, out_tile), lambda i: (0, jnp.clip(i - 2 * steps, 0, outs - 1))),
        scratch_shapes=[pltpu.VMEM((count, 2 * units), jnp.bfloat16)],
        compiler_params=pltpu.CompilerParams(vmem_limit_bytes=56 * 1024 * 1024),
        cost_estimate=pl.CostEstimate(
            flops=12 * count * width * units,
            transcendentals=2 * count * units,
            bytes_accessed=2 * (2 * count * width + 6 * width * units),
        ),
    )(rows, own[0], own[1], other[0], other[1], own[2], other[2])


score_scale = 192.0 ** (-0.5)


def attend_row(query_lat, query_rope, cache_lat, cache_rope, length):
    head_count = query_lat.shape[0]
    rope_width = cache_rope.shape[0]
    scores = lax.dot_general(
        query_lat, cache_lat, (((1,), (1,)), ((), ())), preferred_element_type=jnp.float32
    )
    scores = scores + jnp.dot(
        query_rope.reshape(head_count, rope_width), cache_rope, preferred_element_type=jnp.float32
    )
    scores = scores * score_scale
    positions = jnp.arange(cache_lat.shape[0], dtype=jnp.int32)
    valid = (positions < length)[None, :]
    scores = jnp.where(valid, scores, jnp.float32(-1e30))
    highest = jnp.max(scores, axis=1, keepdims=True)
    weights = jnp.where(valid, jnp.exp(scores - highest), jnp.float32(0.0))
    probs = (weights / jnp.sum(weights, axis=1, keepdims=True)).astype(jnp.bfloat16)
    return jnp.dot(probs, cache_lat, preferred_element_type=jnp.float32).astype(jnp.bfloat16)


def per_device(
    moe_rows,
    expert_ids,
    gate_weights,
    w_gate,
    w_up,
    w_down,
    q_latent,
    q_rope,
    latent_cache,
    rope_cache,
    lengths,
):
    tok_count = moe_rows.shape[0]
    width = moe_rows.shape[1]
    topk_count = expert_ids.shape[1]
    experts = lax.axis_size("dev")
    capacity = min(tok_count, 2 * tok_count * topk_count // experts)
    flat_ids = expert_ids.reshape(-1)
    pair_count = flat_ids.shape[0]
    slot_count = experts * capacity
    one_hot = flat_ids[:, None] == jnp.arange(experts, dtype=jnp.int32)[None, :]
    pair_iota = jnp.arange(pair_count, dtype=jnp.int32)
    lower = (pair_iota[:, None] > pair_iota[None, :]).astype(jnp.bfloat16)
    earlier = jnp.dot(lower, one_hot.astype(jnp.bfloat16), preferred_element_type=jnp.float32)
    slot_index = jnp.sum(jnp.where(one_hot, earlier, 0.0), axis=1).astype(jnp.int32)
    destination = flat_ids * capacity + slot_index
    slot_iota = jnp.arange(slot_count, dtype=jnp.int32)
    picks = destination[:, None] == slot_iota[None, :]
    dispatch = jnp.any(
        destination.reshape(tok_count, topk_count)[None, :, :] == slot_iota[:, None, None], axis=2
    )
    outgoing = jnp.dot(
        dispatch.astype(jnp.bfloat16), moe_rows, preferred_element_type=jnp.float32
    ).astype(jnp.bfloat16).reshape(experts, capacity, width)
    arrived = lax.all_to_all(outgoing, "dev", split_axis=0, concat_axis=0, tiled=True)
    own_rows = arrived.reshape(experts * capacity, width)
    expert_sum = full_expert(own_rows, w_gate, w_up, w_down)
    finished = expert_sum.reshape(experts, capacity, width)
    returned = lax.all_to_all(finished, "dev", split_axis=0, concat_axis=0, tiled=True)
    flat_back = returned.reshape(slot_count, width)
    weighted = jnp.sum(
        jnp.where(picks, gate_weights.reshape(pair_count)[:, None], 0.0).reshape(tok_count, topk_count, slot_count),
        axis=1,
    )
    moe_out = jnp.dot(
        weighted, flat_back.astype(jnp.float32), precision=lax.Precision.HIGHEST,
        preferred_element_type=jnp.float32,
    ).astype(jnp.bfloat16)
    attended = jax.vmap(attend_row)(q_latent, q_rope, latent_cache, rope_cache, lengths)
    return (moe_out, attended)


def solution(mesh):
    placed = (
        P(("role", "dev"), None),
        P(("role", "dev"), None),
        P(("role", "dev"), None),
        P("dev", None, "role"),
        P("dev", None, "role"),
        P("dev", None, "role"),
        P(("role", "dev"), None, None),
        P(("role", "dev"), None),
        P(("role", "dev"), None, None),
        P(("role", "dev"), None, None),
        P(("role", "dev")),
    )
    return jax.shard_map(
        per_device,
        mesh=mesh,
        in_specs=placed,
        out_specs=(P(("role", "dev"), None), P(("role", "dev"), None, None)),
        check_vma=False,
    )
```

```python
import jax
import jax.numpy as jnp
from jax import lax
from jax.sharding import PartitionSpec as P
from jax.experimental import pallas as pl
from jax.experimental.pallas import tpu as pltpu
import functools

def gate_up_kernel(x_ref, g_ref, u_ref, h_ref):
    x = x_ref[...]
    gate_part = jnp.dot(x, g_ref[...], preferred_element_type=jnp.float32)
    up_part = jnp.dot(x, u_ref[...], preferred_element_type=jnp.float32)
    h_ref[...] = (jax.nn.silu(gate_part) * up_part).astype(h_ref.dtype)


def down_kernel(h0_ref, h1_ref, d0_ref, d1_ref, o_ref):
    total = None
    for h_ref, d_ref in ((h0_ref, d0_ref), (h1_ref, d1_ref)):
        term = lax.dot_general(
            h_ref[...], d_ref[...], (((1,), (1,)), ((), ())), preferred_element_type=jnp.float32
        )
        total = term if total is None else total + term
    o_ref[...] = total.astype(o_ref.dtype)


def gate_up(rows, gate_matrix, up_matrix, unit_tile=256):
    count, width = rows.shape
    units = gate_matrix.shape[1]
    return pl.pallas_call(
        gate_up_kernel,
        out_shape=jax.ShapeDtypeStruct((count, units), jnp.bfloat16),
        grid=(units // unit_tile,),
        in_specs=[
            pl.BlockSpec((count, width), lambda j: (0, 0)),
            pl.BlockSpec((width, unit_tile), lambda j: (0, j)),
            pl.BlockSpec((width, unit_tile), lambda j: (0, j)),
        ],
        out_specs=pl.BlockSpec((count, unit_tile), lambda j: (0, j)),
        compiler_params=pltpu.CompilerParams(vmem_limit_bytes=48 * 1024 * 1024),
        cost_estimate=pl.CostEstimate(
            flops=4 * count * width * units,
            transcendentals=count * units,
            bytes_accessed=2 * (count * width + 2 * width * units + count * units),
        ),
    )(rows, gate_matrix, up_matrix)


def down(h0, h1, d0, d1, out_tile=512):
    count, units = h0.shape
    width = d0.shape[0]
    return pl.pallas_call(
        down_kernel,
        out_shape=jax.ShapeDtypeStruct((count, width), jnp.bfloat16),
        grid=(width // out_tile,),
        in_specs=[
            pl.BlockSpec((count, units), lambda j: (0, 0)),
            pl.BlockSpec((count, units), lambda j: (0, 0)),
            pl.BlockSpec((out_tile, units), lambda j: (j, 0)),
            pl.BlockSpec((out_tile, units), lambda j: (j, 0)),
        ],
        out_specs=pl.BlockSpec((count, out_tile), lambda j: (0, j)),
        compiler_params=pltpu.CompilerParams(vmem_limit_bytes=48 * 1024 * 1024),
        cost_estimate=pl.CostEstimate(
            flops=4 * count * width * units,
            transcendentals=0,
            bytes_accessed=2 * (count * width + 2 * width * units + 2 * count * units),
        ),
    )(h0, h1, d0, d1)


def other_half(w):
    return lax.ppermute(w, "role", [(0, 1), (1, 0)])


def ffn_kernel(steps, x_ref, go_ref, uo_ref, gt_ref, ut_ref, do_ref, dt_ref, o_ref, h_ref):
    i = pl.program_id(0)
    tile = go_ref.shape[1]
    units = h_ref.shape[1] // 2

    def hidden(g_ref, u_ref, column):
        x = x_ref[...]
        gate_part = jnp.dot(x, g_ref[...], preferred_element_type=jnp.float32)
        up_part = jnp.dot(x, u_ref[...], preferred_element_type=jnp.float32)
        h_ref[:, pl.ds(pl.multiple_of(column, tile), tile)] = (
            jax.nn.silu(gate_part) * up_part
        ).astype(h_ref.dtype)

    @pl.when(i < steps)
    def _():
        hidden(go_ref, uo_ref, i * tile)

    @pl.when((i >= steps) & (i < 2 * steps))
    def _():
        hidden(gt_ref, ut_ref, units + (i - steps) * tile)

    @pl.when(i >= 2 * steps)
    def _():
        total = lax.dot_general(
            h_ref[:, :units], do_ref[...], (((1,), (1,)), ((), ())), preferred_element_type=jnp.float32
        )
        total = total + lax.dot_general(
            h_ref[:, units:], dt_ref[...], (((1,), (1,)), ((), ())), preferred_element_type=jnp.float32
        )
        o_ref[...] = total.astype(o_ref.dtype)


def full_expert(rows, w_gate, w_up, w_down, unit_tile=256, out_tile=896):
    count, width = rows.shape
    own = (w_gate[0], w_up[0], w_down[0])
    other = tuple(other_half(w) for w in own)
    units = own[0].shape[1]
    steps = units // unit_tile
    outs = width // out_tile

    def own_map(i):
        return (0, jnp.minimum(i, steps - 1))

    def other_map(i):
        return (0, jnp.clip(i - steps, 0, steps - 1))

    def down_map(i):
        return (jnp.clip(i - 2 * steps, 0, outs - 1), 0)

    unit_block = (width, unit_tile)
    return pl.pallas_call(
        functools.partial(ffn_kernel, steps),
        out_shape=jax.ShapeDtypeStruct((count, width), jnp.bfloat16),
        grid=(2 * steps + outs,),
        in_specs=[
            pl.BlockSpec((count, width), lambda i: (0, 0)),
            pl.BlockSpec(unit_block, own_map),
            pl.BlockSpec(unit_block, own_map),
            pl.BlockSpec(unit_block, other_map),
            pl.BlockSpec(unit_block, other_map),
            pl.BlockSpec((out_tile, units), down_map),
            pl.BlockSpec((out_tile, units), down_map),
        ],
        out_specs=pl.BlockSpec((count, out_tile), lambda i: (0, jnp.clip(i - 2 * steps, 0, outs - 1))),
        scratch_shapes=[pltpu.VMEM((count, 2 * units), jnp.bfloat16)],
        compiler_params=pltpu.CompilerParams(vmem_limit_bytes=56 * 1024 * 1024),
        cost_estimate=pl.CostEstimate(
            flops=12 * count * width * units,
            transcendentals=2 * count * units,
            bytes_accessed=2 * (2 * count * width + 6 * width * units),
        ),
    )(rows, own[0], own[1], other[0], other[1], own[2], other[2])


score_scale = 192.0 ** (-0.5)


def attend_row(query_lat, query_rope, cache_lat, cache_rope, length):
    head_count = query_lat.shape[0]
    rope_width = cache_rope.shape[0]
    scores = lax.dot_general(
        query_lat, cache_lat, (((1,), (1,)), ((), ())), preferred_element_type=jnp.float32
    )
    scores = scores + jnp.dot(
        query_rope.reshape(head_count, rope_width), cache_rope, preferred_element_type=jnp.float32
    )
    scores = scores * score_scale
    positions = jnp.arange(cache_lat.shape[0], dtype=jnp.int32)
    valid = (positions < length)[None, :]
    scores = jnp.where(valid, scores, jnp.float32(-1e30))
    highest = jnp.max(scores, axis=1, keepdims=True)
    weights = jnp.where(valid, jnp.exp(scores - highest), jnp.float32(0.0))
    probs = (weights / jnp.sum(weights, axis=1, keepdims=True)).astype(jnp.bfloat16)
    return jnp.dot(probs, cache_lat, preferred_element_type=jnp.float32).astype(jnp.bfloat16)


def per_device(
    moe_rows,
    expert_ids,
    gate_weights,
    w_gate,
    w_up,
    w_down,
    q_latent,
    q_rope,
    latent_cache,
    rope_cache,
    lengths,
):
    tok_count = moe_rows.shape[0]
    width = moe_rows.shape[1]
    topk_count = expert_ids.shape[1]
    experts = lax.axis_size("dev")
    capacity = min(tok_count, 2 * tok_count * topk_count // experts)
    flat_ids = expert_ids.reshape(-1)
    pair_count = flat_ids.shape[0]
    slot_count = experts * capacity
    one_hot = flat_ids[:, None] == jnp.arange(experts, dtype=jnp.int32)[None, :]
    pair_iota = jnp.arange(pair_count, dtype=jnp.int32)
    lower = (pair_iota[:, None] > pair_iota[None, :]).astype(jnp.bfloat16)
    earlier = jnp.dot(lower, one_hot.astype(jnp.bfloat16), preferred_element_type=jnp.float32)
    slot_index = jnp.sum(jnp.where(one_hot, earlier, 0.0), axis=1).astype(jnp.int32)
    destination = flat_ids * capacity + slot_index
    slot_iota = jnp.arange(slot_count, dtype=jnp.int32)
    picks = destination[:, None] == slot_iota[None, :]
    dispatch = jnp.any(
        destination.reshape(tok_count, topk_count)[None, :, :] == slot_iota[:, None, None], axis=2
    )
    outgoing = jnp.dot(
        dispatch.astype(jnp.bfloat16), moe_rows, preferred_element_type=jnp.float32
    ).astype(jnp.bfloat16).reshape(experts, capacity, width)
    arrived = lax.all_to_all(outgoing, "dev", split_axis=0, concat_axis=0, tiled=True)
    own_rows = arrived.reshape(experts * capacity, width)
    expert_sum = full_expert(own_rows, w_gate, w_up, w_down)
    finished = expert_sum.reshape(experts, capacity, width)
    returned = lax.all_to_all(finished, "dev", split_axis=0, concat_axis=0, tiled=True)
    flat_back = returned.reshape(slot_count, width)
    weighted = jnp.sum(
        jnp.where(picks, gate_weights.reshape(pair_count)[:, None], 0.0).reshape(tok_count, topk_count, slot_count),
        axis=1,
    )
    first = weighted.astype(jnp.bfloat16)
    rest = weighted - first.astype(jnp.float32)
    second = rest.astype(jnp.bfloat16)
    third = (rest - second.astype(jnp.float32)).astype(jnp.bfloat16)
    parts = jnp.dot(
        jnp.concatenate([first, second, third], axis=0), flat_back, preferred_element_type=jnp.float32
    )
    moe_out = (parts[:tok_count] + parts[tok_count:2 * tok_count] + parts[2 * tok_count:]).astype(jnp.bfloat16)
    attended = jax.vmap(attend_row)(q_latent, q_rope, latent_cache, rope_cache, lengths)
    return (moe_out, attended)


def solution(mesh):
    placed = (
        P(("role", "dev"), None),
        P(("role", "dev"), None),
        P(("role", "dev"), None),
        P("dev", None, "role"),
        P("dev", None, "role"),
        P("dev", None, "role"),
        P(("role", "dev"), None, None),
        P(("role", "dev"), None),
        P(("role", "dev"), None, None),
        P(("role", "dev"), None, None),
        P(("role", "dev")),
    )
    return jax.shard_map(
        per_device,
        mesh=mesh,
        in_specs=placed,
        out_specs=(P(("role", "dev"), None), P(("role", "dev"), None, None)),
        check_vma=False,
    )
```

```python
import jax
import jax.numpy as jnp
from jax import lax
from jax.sharding import PartitionSpec as P
from jax.experimental import pallas as pl
from jax.experimental.pallas import tpu as pltpu
import functools

def gate_up_kernel(x_ref, g_ref, u_ref, h_ref):
    x = x_ref[...]
    gate_part = jnp.dot(x, g_ref[...], preferred_element_type=jnp.float32)
    up_part = jnp.dot(x, u_ref[...], preferred_element_type=jnp.float32)
    h_ref[...] = (jax.nn.silu(gate_part) * up_part).astype(h_ref.dtype)


def down_kernel(h0_ref, h1_ref, d0_ref, d1_ref, o_ref):
    total = None
    for h_ref, d_ref in ((h0_ref, d0_ref), (h1_ref, d1_ref)):
        term = lax.dot_general(
            h_ref[...], d_ref[...], (((1,), (1,)), ((), ())), preferred_element_type=jnp.float32
        )
        total = term if total is None else total + term
    o_ref[...] = total.astype(o_ref.dtype)


def gate_up(rows, gate_matrix, up_matrix, unit_tile=256):
    count, width = rows.shape
    units = gate_matrix.shape[1]
    return pl.pallas_call(
        gate_up_kernel,
        out_shape=jax.ShapeDtypeStruct((count, units), jnp.bfloat16),
        grid=(units // unit_tile,),
        in_specs=[
            pl.BlockSpec((count, width), lambda j: (0, 0)),
            pl.BlockSpec((width, unit_tile), lambda j: (0, j)),
            pl.BlockSpec((width, unit_tile), lambda j: (0, j)),
        ],
        out_specs=pl.BlockSpec((count, unit_tile), lambda j: (0, j)),
        compiler_params=pltpu.CompilerParams(vmem_limit_bytes=48 * 1024 * 1024),
        cost_estimate=pl.CostEstimate(
            flops=4 * count * width * units,
            transcendentals=count * units,
            bytes_accessed=2 * (count * width + 2 * width * units + count * units),
        ),
    )(rows, gate_matrix, up_matrix)


def down(h0, h1, d0, d1, out_tile=512):
    count, units = h0.shape
    width = d0.shape[0]
    return pl.pallas_call(
        down_kernel,
        out_shape=jax.ShapeDtypeStruct((count, width), jnp.bfloat16),
        grid=(width // out_tile,),
        in_specs=[
            pl.BlockSpec((count, units), lambda j: (0, 0)),
            pl.BlockSpec((count, units), lambda j: (0, 0)),
            pl.BlockSpec((out_tile, units), lambda j: (j, 0)),
            pl.BlockSpec((out_tile, units), lambda j: (j, 0)),
        ],
        out_specs=pl.BlockSpec((count, out_tile), lambda j: (0, j)),
        compiler_params=pltpu.CompilerParams(vmem_limit_bytes=48 * 1024 * 1024),
        cost_estimate=pl.CostEstimate(
            flops=4 * count * width * units,
            transcendentals=0,
            bytes_accessed=2 * (count * width + 2 * width * units + 2 * count * units),
        ),
    )(h0, h1, d0, d1)


MESH = pl.DeviceIdType.MESH

def a2a_kernel(n, x_ref, o_ref, send_sems, recv_sems, local_sem):
    me = lax.axis_index("dev")
    core = lax.axis_index("role")
    local = pltpu.make_async_copy(x_ref.at[me], o_ref.at[me], local_sem)
    local.start()

    def offset_of(k):
        return lax.rem((k - 1) * 2 + me, n - 1) + 1

    def describe(offset):
        peer = lax.rem(me + offset, n)
        return pltpu.make_async_remote_copy(
            src_ref=x_ref.at[peer],
            dst_ref=o_ref.at[me],
            send_sem=send_sems.at[offset],
            recv_sem=recv_sems.at[offset],
            device_id=(core, peer),
            device_id_type=MESH,
        )

    def issue(k, carry):
        describe(offset_of(k)).start()
        return carry

    lax.fori_loop(1, n, issue, 0)

    def finish(offset, carry):
        describe(offset).wait()
        return carry

    lax.fori_loop(1, n, finish, 0)
    local.wait()


def all_to_all_dev(x):
    n = lax.axis_size("dev")
    return pl.pallas_call(
        functools.partial(a2a_kernel, n),
        out_shape=jax.ShapeDtypeStruct(x.shape, x.dtype),
        in_specs=[pl.BlockSpec(memory_space=pltpu.VMEM)],
        out_specs=pl.BlockSpec(memory_space=pltpu.VMEM),
        scratch_shapes=[
            pltpu.SemaphoreType.DMA((n,)),
            pltpu.SemaphoreType.DMA((n,)),
            pltpu.SemaphoreType.DMA(()),
        ],
        compiler_params=pltpu.CompilerParams(has_side_effects=True, vmem_limit_bytes=32 * 1024 * 1024),
    )(x)


score_scale = 192.0 ** (-0.5)


def other_half(w):
    return lax.ppermute(w, "role", [(0, 1), (1, 0)])


def ffn_kernel(steps, x_ref, go_ref, uo_ref, gt_ref, ut_ref, do_ref, dt_ref, o_ref, h_ref):
    i = pl.program_id(0)
    tile = go_ref.shape[1]
    units = h_ref.shape[1] // 2

    def hidden(g_ref, u_ref, column):
        x = x_ref[...]
        gate_part = jnp.dot(x, g_ref[...], preferred_element_type=jnp.float32)
        up_part = jnp.dot(x, u_ref[...], preferred_element_type=jnp.float32)
        h_ref[:, pl.ds(pl.multiple_of(column, tile), tile)] = (
            jax.nn.silu(gate_part) * up_part
        ).astype(h_ref.dtype)

    @pl.when(i < steps)
    def _():
        hidden(go_ref, uo_ref, i * tile)

    @pl.when((i >= steps) & (i < 2 * steps))
    def _():
        hidden(gt_ref, ut_ref, units + (i - steps) * tile)

    @pl.when(i >= 2 * steps)
    def _():
        total = lax.dot_general(
            h_ref[:, :units], do_ref[...], (((1,), (1,)), ((), ())), preferred_element_type=jnp.float32
        )
        total = total + lax.dot_general(
            h_ref[:, units:], dt_ref[...], (((1,), (1,)), ((), ())), preferred_element_type=jnp.float32
        )
        o_ref[...] = total.astype(o_ref.dtype)


def full_expert(rows, w_gate, w_up, w_down, unit_tile=256, out_tile=896):
    count, width = rows.shape
    own = (w_gate[0], w_up[0], w_down[0])
    other = tuple(other_half(w) for w in own)
    units = own[0].shape[1]
    steps = units // unit_tile
    outs = width // out_tile

    def own_map(i):
        return (0, jnp.minimum(i, steps - 1))

    def other_map(i):
        return (0, jnp.clip(i - steps, 0, steps - 1))

    def down_map(i):
        return (jnp.clip(i - 2 * steps, 0, outs - 1), 0)

    unit_block = (width, unit_tile)
    return pl.pallas_call(
        functools.partial(ffn_kernel, steps),
        out_shape=jax.ShapeDtypeStruct((count, width), jnp.bfloat16),
        grid=(2 * steps + outs,),
        in_specs=[
            pl.BlockSpec((count, width), lambda i: (0, 0)),
            pl.BlockSpec(unit_block, own_map),
            pl.BlockSpec(unit_block, own_map),
            pl.BlockSpec(unit_block, other_map),
            pl.BlockSpec(unit_block, other_map),
            pl.BlockSpec((out_tile, units), down_map),
            pl.BlockSpec((out_tile, units), down_map),
        ],
        out_specs=pl.BlockSpec((count, out_tile), lambda i: (0, jnp.clip(i - 2 * steps, 0, outs - 1))),
        scratch_shapes=[pltpu.VMEM((count, 2 * units), jnp.bfloat16)],
        compiler_params=pltpu.CompilerParams(vmem_limit_bytes=56 * 1024 * 1024),
        cost_estimate=pl.CostEstimate(
            flops=12 * count * width * units,
            transcendentals=2 * count * units,
            bytes_accessed=2 * (2 * count * width + 6 * width * units),
        ),
    )(rows, own[0], own[1], other[0], other[1], own[2], other[2])


score_scale = 192.0 ** (-0.5)


def attend_row(query_lat, query_rope, cache_lat, cache_rope, length):
    head_count = query_lat.shape[0]
    rope_width = cache_rope.shape[0]
    scores = lax.dot_general(
        query_lat, cache_lat, (((1,), (1,)), ((), ())), preferred_element_type=jnp.float32
    )
    scores = scores + jnp.dot(
        query_rope.reshape(head_count, rope_width), cache_rope, preferred_element_type=jnp.float32
    )
    scores = scores * score_scale
    positions = jnp.arange(cache_lat.shape[0], dtype=jnp.int32)
    valid = (positions < length)[None, :]
    scores = jnp.where(valid, scores, jnp.float32(-1e30))
    highest = jnp.max(scores, axis=1, keepdims=True)
    weights = jnp.where(valid, jnp.exp(scores - highest), jnp.float32(0.0))
    probs = (weights / jnp.sum(weights, axis=1, keepdims=True)).astype(jnp.bfloat16)
    return jnp.dot(probs, cache_lat, preferred_element_type=jnp.float32).astype(jnp.bfloat16)


def per_device(
    moe_rows,
    expert_ids,
    gate_weights,
    w_gate,
    w_up,
    w_down,
    q_latent,
    q_rope,
    latent_cache,
    rope_cache,
    lengths,
):
    tok_count = moe_rows.shape[0]
    width = moe_rows.shape[1]
    topk_count = expert_ids.shape[1]
    experts = lax.axis_size("dev")
    capacity = min(tok_count, 2 * tok_count * topk_count // experts)
    flat_ids = expert_ids.reshape(-1)
    pair_count = flat_ids.shape[0]
    slot_count = experts * capacity
    one_hot = flat_ids[:, None] == jnp.arange(experts, dtype=jnp.int32)[None, :]
    pair_iota = jnp.arange(pair_count, dtype=jnp.int32)
    lower = (pair_iota[:, None] > pair_iota[None, :]).astype(jnp.bfloat16)
    earlier = jnp.dot(lower, one_hot.astype(jnp.bfloat16), preferred_element_type=jnp.float32)
    slot_index = jnp.sum(jnp.where(one_hot, earlier, 0.0), axis=1).astype(jnp.int32)
    destination = flat_ids * capacity + slot_index
    slot_iota = jnp.arange(slot_count, dtype=jnp.int32)
    picks = destination[:, None] == slot_iota[None, :]
    dispatch = jnp.any(
        destination.reshape(tok_count, topk_count)[None, :, :] == slot_iota[:, None, None], axis=2
    )
    outgoing = jnp.dot(
        dispatch.astype(jnp.bfloat16), moe_rows, preferred_element_type=jnp.float32
    ).astype(jnp.bfloat16).reshape(experts, capacity, width)
    arrived = all_to_all_dev(outgoing)
    own_rows = arrived.reshape(experts * capacity, width)
    expert_sum = full_expert(own_rows, w_gate, w_up, w_down)
    finished = expert_sum.reshape(experts, capacity, width)
    returned = lax.all_to_all(finished, "dev", split_axis=0, concat_axis=0, tiled=True)
    flat_back = returned.reshape(slot_count, width)
    weighted = jnp.sum(
        jnp.where(picks, gate_weights.reshape(pair_count)[:, None], 0.0).reshape(tok_count, topk_count, slot_count),
        axis=1,
    )
    moe_out = jnp.dot(
        weighted, flat_back.astype(jnp.float32), precision=lax.Precision.HIGHEST,
        preferred_element_type=jnp.float32,
    ).astype(jnp.bfloat16)
    attended = jax.vmap(attend_row)(q_latent, q_rope, latent_cache, rope_cache, lengths)
    return (moe_out, attended)


def solution(mesh):
    placed = (
        P(("role", "dev"), None),
        P(("role", "dev"), None),
        P(("role", "dev"), None),
        P("dev", None, "role"),
        P("dev", None, "role"),
        P("dev", None, "role"),
        P(("role", "dev"), None, None),
        P(("role", "dev"), None),
        P(("role", "dev"), None, None),
        P(("role", "dev"), None, None),
        P(("role", "dev")),
    )
    return jax.shard_map(
        per_device,
        mesh=mesh,
        in_specs=placed,
        out_specs=(P(("role", "dev"), None), P(("role", "dev"), None, None)),
        check_vma=False,
    )
```

```python
import jax
import jax.numpy as jnp
from jax import lax
from jax.sharding import PartitionSpec as P
from jax.experimental import pallas as pl
from jax.experimental.pallas import tpu as pltpu
import functools

def gate_up_kernel(x_ref, g_ref, u_ref, h_ref):
    x = x_ref[...]
    gate_part = jnp.dot(x, g_ref[...], preferred_element_type=jnp.float32)
    up_part = jnp.dot(x, u_ref[...], preferred_element_type=jnp.float32)
    h_ref[...] = (jax.nn.silu(gate_part) * up_part).astype(h_ref.dtype)


def down_kernel(h0_ref, h1_ref, d0_ref, d1_ref, o_ref):
    total = None
    for h_ref, d_ref in ((h0_ref, d0_ref), (h1_ref, d1_ref)):
        term = lax.dot_general(
            h_ref[...], d_ref[...], (((1,), (1,)), ((), ())), preferred_element_type=jnp.float32
        )
        total = term if total is None else total + term
    o_ref[...] = total.astype(o_ref.dtype)


def gate_up(rows, gate_matrix, up_matrix, unit_tile=256):
    count, width = rows.shape
    units = gate_matrix.shape[1]
    return pl.pallas_call(
        gate_up_kernel,
        out_shape=jax.ShapeDtypeStruct((count, units), jnp.bfloat16),
        grid=(units // unit_tile,),
        in_specs=[
            pl.BlockSpec((count, width), lambda j: (0, 0)),
            pl.BlockSpec((width, unit_tile), lambda j: (0, j)),
            pl.BlockSpec((width, unit_tile), lambda j: (0, j)),
        ],
        out_specs=pl.BlockSpec((count, unit_tile), lambda j: (0, j)),
        compiler_params=pltpu.CompilerParams(vmem_limit_bytes=48 * 1024 * 1024),
        cost_estimate=pl.CostEstimate(
            flops=4 * count * width * units,
            transcendentals=count * units,
            bytes_accessed=2 * (count * width + 2 * width * units + count * units),
        ),
    )(rows, gate_matrix, up_matrix)


def down(h0, h1, d0, d1, out_tile=512):
    count, units = h0.shape
    width = d0.shape[0]
    return pl.pallas_call(
        down_kernel,
        out_shape=jax.ShapeDtypeStruct((count, width), jnp.bfloat16),
        grid=(width // out_tile,),
        in_specs=[
            pl.BlockSpec((count, units), lambda j: (0, 0)),
            pl.BlockSpec((count, units), lambda j: (0, 0)),
            pl.BlockSpec((out_tile, units), lambda j: (j, 0)),
            pl.BlockSpec((out_tile, units), lambda j: (j, 0)),
        ],
        out_specs=pl.BlockSpec((count, out_tile), lambda j: (0, j)),
        compiler_params=pltpu.CompilerParams(vmem_limit_bytes=48 * 1024 * 1024),
        cost_estimate=pl.CostEstimate(
            flops=4 * count * width * units,
            transcendentals=0,
            bytes_accessed=2 * (count * width + 2 * width * units + 2 * count * units),
        ),
    )(h0, h1, d0, d1)


def other_half(w):
    return lax.ppermute(w, "role", [(0, 1), (1, 0)])


def ffn_kernel(steps, x_ref, go_ref, uo_ref, gt_ref, ut_ref, do_ref, dt_ref, o_ref, h_ref):
    i = pl.program_id(0)
    tile = go_ref.shape[1]
    units = h_ref.shape[1] // 2

    def hidden(g_ref, u_ref, column):
        x = x_ref[...]
        gate_part = jnp.dot(x, g_ref[...], preferred_element_type=jnp.float32)
        up_part = jnp.dot(x, u_ref[...], preferred_element_type=jnp.float32)
        h_ref[:, pl.ds(pl.multiple_of(column, tile), tile)] = (
            jax.nn.silu(gate_part) * up_part
        ).astype(h_ref.dtype)

    @pl.when(i < steps)
    def _():
        hidden(go_ref, uo_ref, i * tile)

    @pl.when((i >= steps) & (i < 2 * steps))
    def _():
        hidden(gt_ref, ut_ref, units + (i - steps) * tile)

    @pl.when(i >= 2 * steps)
    def _():
        total = lax.dot_general(
            h_ref[:, :units], do_ref[...], (((1,), (1,)), ((), ())), preferred_element_type=jnp.float32
        )
        total = total + lax.dot_general(
            h_ref[:, units:], dt_ref[...], (((1,), (1,)), ((), ())), preferred_element_type=jnp.float32
        )
        o_ref[...] = total.astype(o_ref.dtype)


def full_expert(rows, w_gate, w_up, w_down, unit_tile=256, out_tile=896):
    count, width = rows.shape
    own = (w_gate[0], w_up[0], w_down[0])
    other = tuple(other_half(w) for w in own)
    units = own[0].shape[1]
    steps = units // unit_tile
    outs = width // out_tile

    def own_map(i):
        return (0, jnp.minimum(i, steps - 1))

    def other_map(i):
        return (0, jnp.clip(i - steps, 0, steps - 1))

    def down_map(i):
        return (jnp.clip(i - 2 * steps, 0, outs - 1), 0)

    unit_block = (width, unit_tile)
    return pl.pallas_call(
        functools.partial(ffn_kernel, steps),
        out_shape=jax.ShapeDtypeStruct((count, width), jnp.bfloat16),
        grid=(2 * steps + outs,),
        in_specs=[
            pl.BlockSpec((count, width), lambda i: (0, 0)),
            pl.BlockSpec(unit_block, own_map),
            pl.BlockSpec(unit_block, own_map),
            pl.BlockSpec(unit_block, other_map),
            pl.BlockSpec(unit_block, other_map),
            pl.BlockSpec((out_tile, units), down_map),
            pl.BlockSpec((out_tile, units), down_map),
        ],
        out_specs=pl.BlockSpec((count, out_tile), lambda i: (0, jnp.clip(i - 2 * steps, 0, outs - 1))),
        scratch_shapes=[pltpu.VMEM((count, 2 * units), jnp.bfloat16)],
        compiler_params=pltpu.CompilerParams(vmem_limit_bytes=56 * 1024 * 1024),
        cost_estimate=pl.CostEstimate(
            flops=12 * count * width * units,
            transcendentals=2 * count * units,
            bytes_accessed=2 * (2 * count * width + 6 * width * units),
        ),
    )(rows, own[0], own[1], other[0], other[1], own[2], other[2])


score_scale = 192.0 ** (-0.5)


def attend_row(query_lat, query_rope, cache_lat, cache_rope, length):
    head_count = query_lat.shape[0]
    rope_width = cache_rope.shape[0]
    scores = lax.dot_general(
        query_lat, cache_lat, (((1,), (1,)), ((), ())), preferred_element_type=jnp.float32
    )
    scores = scores + jnp.dot(
        query_rope.reshape(head_count, rope_width), cache_rope, preferred_element_type=jnp.float32
    )
    scores = scores * score_scale
    positions = jnp.arange(cache_lat.shape[0], dtype=jnp.int32)
    valid = (positions < length)[None, :]
    scores = jnp.where(valid, scores, jnp.float32(-1e30))
    highest = jnp.max(scores, axis=1, keepdims=True)
    weights = jnp.where(valid, jnp.exp(scores - highest), jnp.float32(0.0))
    probs = (weights / jnp.sum(weights, axis=1, keepdims=True)).astype(jnp.bfloat16)
    return jnp.dot(probs, cache_lat, preferred_element_type=jnp.float32).astype(jnp.bfloat16)


def per_device(
    moe_rows,
    expert_ids,
    gate_weights,
    w_gate,
    w_up,
    w_down,
    q_latent,
    q_rope,
    latent_cache,
    rope_cache,
    lengths,
):
    tok_count = moe_rows.shape[0]
    width = moe_rows.shape[1]
    topk_count = expert_ids.shape[1]
    experts = lax.axis_size("dev")
    capacity = min(tok_count, 2 * tok_count * topk_count // experts)
    flat_ids = expert_ids.reshape(-1)
    pair_count = flat_ids.shape[0]
    slot_count = experts * capacity
    one_hot = flat_ids[:, None] == jnp.arange(experts, dtype=jnp.int32)[None, :]
    pair_iota = jnp.arange(pair_count, dtype=jnp.int32)
    lower = (pair_iota[:, None] > pair_iota[None, :]).astype(jnp.bfloat16)
    earlier = jnp.dot(lower, one_hot.astype(jnp.bfloat16), preferred_element_type=jnp.float32)
    slot_index = jnp.sum(jnp.where(one_hot, earlier, 0.0), axis=1).astype(jnp.int32)
    destination = flat_ids * capacity + slot_index
    slot_iota = jnp.arange(slot_count, dtype=jnp.int32)
    picks = destination[:, None] == slot_iota[None, :]
    dispatch = jnp.any(
        destination.reshape(tok_count, topk_count)[None, :, :] == slot_iota[:, None, None], axis=2
    )
    outgoing = jnp.dot(
        dispatch.astype(jnp.bfloat16), moe_rows, preferred_element_type=jnp.float32
    ).astype(jnp.bfloat16).reshape(experts, capacity, width)
    arrived = lax.all_to_all(outgoing, "dev", split_axis=0, concat_axis=0, tiled=True)
    own_rows = arrived.reshape(experts * capacity, width)
    expert_sum = full_expert(own_rows, w_gate, w_up, w_down)
    finished = expert_sum.reshape(experts, capacity, width)
    returned = lax.all_to_all(finished, "dev", split_axis=0, concat_axis=0, tiled=True)
    flat_back = returned.reshape(slot_count, width)
    weighted = jnp.sum(
        jnp.where(picks, gate_weights.reshape(pair_count)[:, None], 0.0).reshape(tok_count, topk_count, slot_count),
        axis=1,
    )
    first = lax.reduce_precision(weighted, exponent_bits=8, mantissa_bits=7)
    rest = weighted - first
    second = lax.reduce_precision(rest, exponent_bits=8, mantissa_bits=7)
    parts = [first, second, rest - second]
    split = jnp.concatenate([part.astype(jnp.bfloat16) for part in parts], axis=0)
    sums = jnp.dot(split, flat_back, preferred_element_type=jnp.float32)
    moe_out = (sums[:tok_count] + sums[tok_count:2 * tok_count] + sums[2 * tok_count:]).astype(jnp.bfloat16)
    attended = jax.vmap(attend_row)(q_latent, q_rope, latent_cache, rope_cache, lengths)
    return (moe_out, attended)


def solution(mesh):
    placed = (
        P(("role", "dev"), None),
        P(("role", "dev"), None),
        P(("role", "dev"), None),
        P("dev", None, "role"),
        P("dev", None, "role"),
        P("dev", None, "role"),
        P(("role", "dev"), None, None),
        P(("role", "dev"), None),
        P(("role", "dev"), None, None),
        P(("role", "dev"), None, None),
        P(("role", "dev")),
    )
    return jax.shard_map(
        per_device,
        mesh=mesh,
        in_specs=placed,
        out_specs=(P(("role", "dev"), None), P(("role", "dev"), None, None)),
        check_vma=False,
    )
```

```python
import jax
import jax.numpy as jnp
from jax import lax
from jax.sharding import PartitionSpec as P
from jax.experimental import pallas as pl
from jax.experimental.pallas import tpu as pltpu
import functools

def gate_up_kernel(x_ref, g_ref, u_ref, h_ref):
    x = x_ref[...]
    gate_part = jnp.dot(x, g_ref[...], preferred_element_type=jnp.float32)
    up_part = jnp.dot(x, u_ref[...], preferred_element_type=jnp.float32)
    h_ref[...] = (jax.nn.silu(gate_part) * up_part).astype(h_ref.dtype)


def down_kernel(h0_ref, h1_ref, d0_ref, d1_ref, o_ref):
    total = None
    for h_ref, d_ref in ((h0_ref, d0_ref), (h1_ref, d1_ref)):
        term = lax.dot_general(
            h_ref[...], d_ref[...], (((1,), (1,)), ((), ())), preferred_element_type=jnp.float32
        )
        total = term if total is None else total + term
    o_ref[...] = total.astype(o_ref.dtype)


def gate_up(rows, gate_matrix, up_matrix, unit_tile=256):
    count, width = rows.shape
    units = gate_matrix.shape[1]
    return pl.pallas_call(
        gate_up_kernel,
        out_shape=jax.ShapeDtypeStruct((count, units), jnp.bfloat16),
        grid=(units // unit_tile,),
        in_specs=[
            pl.BlockSpec((count, width), lambda j: (0, 0)),
            pl.BlockSpec((width, unit_tile), lambda j: (0, j)),
            pl.BlockSpec((width, unit_tile), lambda j: (0, j)),
        ],
        out_specs=pl.BlockSpec((count, unit_tile), lambda j: (0, j)),
        compiler_params=pltpu.CompilerParams(vmem_limit_bytes=48 * 1024 * 1024),
        cost_estimate=pl.CostEstimate(
            flops=4 * count * width * units,
            transcendentals=count * units,
            bytes_accessed=2 * (count * width + 2 * width * units + count * units),
        ),
    )(rows, gate_matrix, up_matrix)


def down(h0, h1, d0, d1, out_tile=512):
    count, units = h0.shape
    width = d0.shape[0]
    return pl.pallas_call(
        down_kernel,
        out_shape=jax.ShapeDtypeStruct((count, width), jnp.bfloat16),
        grid=(width // out_tile,),
        in_specs=[
            pl.BlockSpec((count, units), lambda j: (0, 0)),
            pl.BlockSpec((count, units), lambda j: (0, 0)),
            pl.BlockSpec((out_tile, units), lambda j: (j, 0)),
            pl.BlockSpec((out_tile, units), lambda j: (j, 0)),
        ],
        out_specs=pl.BlockSpec((count, out_tile), lambda j: (0, j)),
        compiler_params=pltpu.CompilerParams(vmem_limit_bytes=48 * 1024 * 1024),
        cost_estimate=pl.CostEstimate(
            flops=4 * count * width * units,
            transcendentals=0,
            bytes_accessed=2 * (count * width + 2 * width * units + 2 * count * units),
        ),
    )(h0, h1, d0, d1)


def other_half(w):
    return lax.ppermute(w, "role", [(0, 1), (1, 0)])


def ffn_kernel(steps, x_ref, go_ref, uo_ref, gt_ref, ut_ref, do_ref, dt_ref, o_ref, h_ref):
    i = pl.program_id(0)
    tile = go_ref.shape[1]
    units = h_ref.shape[1] // 2

    def hidden(g_ref, u_ref, column):
        x = x_ref[...]
        gate_part = jnp.dot(x, g_ref[...], preferred_element_type=jnp.float32)
        up_part = jnp.dot(x, u_ref[...], preferred_element_type=jnp.float32)
        h_ref[:, pl.ds(pl.multiple_of(column, tile), tile)] = (
            jax.nn.silu(gate_part) * up_part
        ).astype(h_ref.dtype)

    @pl.when(i < steps)
    def _():
        hidden(go_ref, uo_ref, i * tile)

    @pl.when((i >= steps) & (i < 2 * steps))
    def _():
        hidden(gt_ref, ut_ref, units + (i - steps) * tile)

    @pl.when(i >= 2 * steps)
    def _():
        total = lax.dot_general(
            h_ref[:, :units], do_ref[...], (((1,), (1,)), ((), ())), preferred_element_type=jnp.float32
        )
        total = total + lax.dot_general(
            h_ref[:, units:], dt_ref[...], (((1,), (1,)), ((), ())), preferred_element_type=jnp.float32
        )
        o_ref[...] = total.astype(o_ref.dtype)


def full_expert(rows, w_gate, w_up, w_down, unit_tile=256, out_tile=1792):
    count, width = rows.shape
    own = (w_gate[0], w_up[0], w_down[0])
    other = tuple(other_half(w) for w in own)
    units = own[0].shape[1]
    steps = units // unit_tile
    outs = width // out_tile

    def own_map(i):
        return (0, jnp.minimum(i, steps - 1))

    def other_map(i):
        return (0, jnp.clip(i - steps, 0, steps - 1))

    def down_map(i):
        return (jnp.clip(i - 2 * steps, 0, outs - 1), 0)

    unit_block = (width, unit_tile)
    return pl.pallas_call(
        functools.partial(ffn_kernel, steps),
        out_shape=jax.ShapeDtypeStruct((count, width), jnp.bfloat16),
        grid=(2 * steps + outs,),
        in_specs=[
            pl.BlockSpec((count, width), lambda i: (0, 0)),
            pl.BlockSpec(unit_block, own_map),
            pl.BlockSpec(unit_block, own_map),
            pl.BlockSpec(unit_block, other_map),
            pl.BlockSpec(unit_block, other_map),
            pl.BlockSpec((out_tile, units), down_map),
            pl.BlockSpec((out_tile, units), down_map),
        ],
        out_specs=pl.BlockSpec((count, out_tile), lambda i: (0, jnp.clip(i - 2 * steps, 0, outs - 1))),
        scratch_shapes=[pltpu.VMEM((count, 2 * units), jnp.bfloat16)],
        compiler_params=pltpu.CompilerParams(vmem_limit_bytes=56 * 1024 * 1024),
        cost_estimate=pl.CostEstimate(
            flops=12 * count * width * units,
            transcendentals=2 * count * units,
            bytes_accessed=2 * (2 * count * width + 6 * width * units),
        ),
    )(rows, own[0], own[1], other[0], other[1], own[2], other[2])


score_scale = 192.0 ** (-0.5)


def attend_row(query_lat, query_rope, cache_lat, cache_rope, length):
    head_count = query_lat.shape[0]
    rope_width = cache_rope.shape[0]
    scores = lax.dot_general(
        query_lat, cache_lat, (((1,), (1,)), ((), ())), preferred_element_type=jnp.float32
    )
    scores = scores + jnp.dot(
        query_rope.reshape(head_count, rope_width), cache_rope, preferred_element_type=jnp.float32
    )
    scores = scores * score_scale
    positions = jnp.arange(cache_lat.shape[0], dtype=jnp.int32)
    valid = (positions < length)[None, :]
    scores = jnp.where(valid, scores, jnp.float32(-1e30))
    highest = jnp.max(scores, axis=1, keepdims=True)
    weights = jnp.where(valid, jnp.exp(scores - highest), jnp.float32(0.0))
    probs = (weights / jnp.sum(weights, axis=1, keepdims=True)).astype(jnp.bfloat16)
    return jnp.dot(probs, cache_lat, preferred_element_type=jnp.float32).astype(jnp.bfloat16)


def per_device(
    moe_rows,
    expert_ids,
    gate_weights,
    w_gate,
    w_up,
    w_down,
    q_latent,
    q_rope,
    latent_cache,
    rope_cache,
    lengths,
):
    tok_count = moe_rows.shape[0]
    width = moe_rows.shape[1]
    topk_count = expert_ids.shape[1]
    experts = lax.axis_size("dev")
    capacity = min(tok_count, 2 * tok_count * topk_count // experts)
    flat_ids = expert_ids.reshape(-1)
    pair_count = flat_ids.shape[0]
    slot_count = experts * capacity
    one_hot = flat_ids[:, None] == jnp.arange(experts, dtype=jnp.int32)[None, :]
    pair_iota = jnp.arange(pair_count, dtype=jnp.int32)
    lower = (pair_iota[:, None] > pair_iota[None, :]).astype(jnp.bfloat16)
    earlier = jnp.dot(lower, one_hot.astype(jnp.bfloat16), preferred_element_type=jnp.float32)
    slot_index = jnp.sum(jnp.where(one_hot, earlier, 0.0), axis=1).astype(jnp.int32)
    destination = flat_ids * capacity + slot_index
    slot_iota = jnp.arange(slot_count, dtype=jnp.int32)
    picks = destination[:, None] == slot_iota[None, :]
    dispatch = jnp.any(
        destination.reshape(tok_count, topk_count)[None, :, :] == slot_iota[:, None, None], axis=2
    )
    outgoing = jnp.dot(
        dispatch.astype(jnp.bfloat16), moe_rows, preferred_element_type=jnp.float32
    ).astype(jnp.bfloat16).reshape(experts, capacity, width)
    arrived = lax.all_to_all(outgoing, "dev", split_axis=0, concat_axis=0, tiled=True)
    own_rows = arrived.reshape(experts * capacity, width)
    expert_sum = full_expert(own_rows, w_gate, w_up, w_down)
    finished = expert_sum.reshape(experts, capacity, width)
    returned = lax.all_to_all(finished, "dev", split_axis=0, concat_axis=0, tiled=True)
    flat_back = returned.reshape(slot_count, width)
    weighted = jnp.sum(
        jnp.where(picks, gate_weights.reshape(pair_count)[:, None], 0.0).reshape(tok_count, topk_count, slot_count),
        axis=1,
    )
    first = lax.reduce_precision(weighted, exponent_bits=8, mantissa_bits=7)
    rest = weighted - first
    second = lax.reduce_precision(rest, exponent_bits=8, mantissa_bits=7)
    parts = [first, second, rest - second]
    split = jnp.concatenate([part.astype(jnp.bfloat16) for part in parts], axis=0)
    sums = jnp.dot(split, flat_back, preferred_element_type=jnp.float32)
    moe_out = (sums[:tok_count] + sums[tok_count:2 * tok_count] + sums[2 * tok_count:]).astype(jnp.bfloat16)
    attended = jax.vmap(attend_row)(q_latent, q_rope, latent_cache, rope_cache, lengths)
    return (moe_out, attended)


def solution(mesh):
    placed = (
        P(("role", "dev"), None),
        P(("role", "dev"), None),
        P(("role", "dev"), None),
        P("dev", None, "role"),
        P("dev", None, "role"),
        P("dev", None, "role"),
        P(("role", "dev"), None, None),
        P(("role", "dev"), None),
        P(("role", "dev"), None, None),
        P(("role", "dev"), None, None),
        P(("role", "dev")),
    )
    return jax.shard_map(
        per_device,
        mesh=mesh,
        in_specs=placed,
        out_specs=(P(("role", "dev"), None), P(("role", "dev"), None, None)),
        check_vma=False,
    )
```

```python
import jax
import jax.numpy as jnp
from jax import lax
from jax.sharding import PartitionSpec as P
from jax.experimental import pallas as pl
from jax.experimental.pallas import tpu as pltpu
import functools

def gate_up_kernel(x_ref, g_ref, u_ref, h_ref):
    x = x_ref[...]
    gate_part = jnp.dot(x, g_ref[...], preferred_element_type=jnp.float32)
    up_part = jnp.dot(x, u_ref[...], preferred_element_type=jnp.float32)
    h_ref[...] = (jax.nn.silu(gate_part) * up_part).astype(h_ref.dtype)


def down_kernel(h0_ref, h1_ref, d0_ref, d1_ref, o_ref):
    total = None
    for h_ref, d_ref in ((h0_ref, d0_ref), (h1_ref, d1_ref)):
        term = lax.dot_general(
            h_ref[...], d_ref[...], (((1,), (1,)), ((), ())), preferred_element_type=jnp.float32
        )
        total = term if total is None else total + term
    o_ref[...] = total.astype(o_ref.dtype)


def gate_up(rows, gate_matrix, up_matrix, unit_tile=256):
    count, width = rows.shape
    units = gate_matrix.shape[1]
    return pl.pallas_call(
        gate_up_kernel,
        out_shape=jax.ShapeDtypeStruct((count, units), jnp.bfloat16),
        grid=(units // unit_tile,),
        in_specs=[
            pl.BlockSpec((count, width), lambda j: (0, 0)),
            pl.BlockSpec((width, unit_tile), lambda j: (0, j)),
            pl.BlockSpec((width, unit_tile), lambda j: (0, j)),
        ],
        out_specs=pl.BlockSpec((count, unit_tile), lambda j: (0, j)),
        compiler_params=pltpu.CompilerParams(vmem_limit_bytes=48 * 1024 * 1024),
        cost_estimate=pl.CostEstimate(
            flops=4 * count * width * units,
            transcendentals=count * units,
            bytes_accessed=2 * (count * width + 2 * width * units + count * units),
        ),
    )(rows, gate_matrix, up_matrix)


def down(h0, h1, d0, d1, out_tile=512):
    count, units = h0.shape
    width = d0.shape[0]
    return pl.pallas_call(
        down_kernel,
        out_shape=jax.ShapeDtypeStruct((count, width), jnp.bfloat16),
        grid=(width // out_tile,),
        in_specs=[
            pl.BlockSpec((count, units), lambda j: (0, 0)),
            pl.BlockSpec((count, units), lambda j: (0, 0)),
            pl.BlockSpec((out_tile, units), lambda j: (j, 0)),
            pl.BlockSpec((out_tile, units), lambda j: (j, 0)),
        ],
        out_specs=pl.BlockSpec((count, out_tile), lambda j: (0, j)),
        compiler_params=pltpu.CompilerParams(vmem_limit_bytes=48 * 1024 * 1024),
        cost_estimate=pl.CostEstimate(
            flops=4 * count * width * units,
            transcendentals=0,
            bytes_accessed=2 * (count * width + 2 * width * units + 2 * count * units),
        ),
    )(h0, h1, d0, d1)


def other_half(w):
    return lax.ppermute(w, "role", [(0, 1), (1, 0)])


def ffn_kernel(steps, x_ref, go_ref, uo_ref, gt_ref, ut_ref, do_ref, dt_ref, o_ref, h_ref):
    i = pl.program_id(0)
    tile = go_ref.shape[1]
    units = h_ref.shape[1] // 2

    def hidden(g_ref, u_ref, column):
        x = x_ref[...]
        gate_part = jnp.dot(x, g_ref[...], preferred_element_type=jnp.float32)
        up_part = jnp.dot(x, u_ref[...], preferred_element_type=jnp.float32)
        h_ref[:, pl.ds(pl.multiple_of(column, tile), tile)] = (
            jax.nn.silu(gate_part) * up_part
        ).astype(h_ref.dtype)

    @pl.when(i < steps)
    def _():
        hidden(go_ref, uo_ref, i * tile)

    @pl.when((i >= steps) & (i < 2 * steps))
    def _():
        hidden(gt_ref, ut_ref, units + (i - steps) * tile)

    @pl.when(i >= 2 * steps)
    def _():
        total = lax.dot_general(
            h_ref[:, :units], do_ref[...], (((1,), (1,)), ((), ())), preferred_element_type=jnp.float32
        )
        total = total + lax.dot_general(
            h_ref[:, units:], dt_ref[...], (((1,), (1,)), ((), ())), preferred_element_type=jnp.float32
        )
        o_ref[...] = total.astype(o_ref.dtype)


def full_expert(rows, w_gate, w_up, w_down, unit_tile=256, out_tile=1792):
    count, width = rows.shape
    own = (w_gate[0], w_up[0], w_down[0])
    other = tuple(other_half(w) for w in own)
    units = own[0].shape[1]
    steps = units // unit_tile
    outs = width // out_tile

    def own_map(i):
        return (0, jnp.minimum(i, steps - 1))

    def other_map(i):
        return (0, jnp.clip(i - steps, 0, steps - 1))

    def down_map(i):
        return (jnp.clip(i - 2 * steps, 0, outs - 1), 0)

    unit_block = (width, unit_tile)
    return pl.pallas_call(
        functools.partial(ffn_kernel, steps),
        out_shape=jax.ShapeDtypeStruct((count, width), jnp.bfloat16),
        grid=(2 * steps + outs,),
        in_specs=[
            pl.BlockSpec((count, width), lambda i: (0, 0)),
            pl.BlockSpec(unit_block, own_map),
            pl.BlockSpec(unit_block, own_map),
            pl.BlockSpec(unit_block, other_map),
            pl.BlockSpec(unit_block, other_map),
            pl.BlockSpec((out_tile, units), down_map),
            pl.BlockSpec((out_tile, units), down_map),
        ],
        out_specs=pl.BlockSpec((count, out_tile), lambda i: (0, jnp.clip(i - 2 * steps, 0, outs - 1))),
        scratch_shapes=[pltpu.VMEM((count, 2 * units), jnp.bfloat16)],
        compiler_params=pltpu.CompilerParams(vmem_limit_bytes=56 * 1024 * 1024),
        cost_estimate=pl.CostEstimate(
            flops=12 * count * width * units,
            transcendentals=2 * count * units,
            bytes_accessed=2 * (2 * count * width + 6 * width * units),
        ),
    )(rows, own[0], own[1], other[0], other[1], own[2], other[2])


score_scale = 192.0 ** (-0.5)


def attend_row(query_lat, query_rope, cache_lat, cache_rope, length):
    head_count = query_lat.shape[0]
    rope_width = cache_rope.shape[0]
    scores = lax.dot_general(
        query_lat, cache_lat, (((1,), (1,)), ((), ())), preferred_element_type=jnp.float32
    )
    scores = scores + jnp.dot(
        query_rope.reshape(head_count, rope_width), cache_rope, preferred_element_type=jnp.float32
    )
    scores = scores * score_scale
    positions = jnp.arange(cache_lat.shape[0], dtype=jnp.int32)
    valid = (positions < length)[None, :]
    scores = jnp.where(valid, scores, jnp.float32(-1e30))
    highest = jnp.max(scores, axis=1, keepdims=True)
    weights = jnp.where(valid, jnp.exp(scores - highest), jnp.float32(0.0))
    probs = (weights / jnp.sum(weights, axis=1, keepdims=True)).astype(jnp.bfloat16)
    return jnp.dot(probs, cache_lat, preferred_element_type=jnp.float32).astype(jnp.bfloat16)


def per_device(
    moe_rows,
    expert_ids,
    gate_weights,
    w_gate,
    w_up,
    w_down,
    q_latent,
    q_rope,
    latent_cache,
    rope_cache,
    lengths,
):
    tok_count = moe_rows.shape[0]
    width = moe_rows.shape[1]
    topk_count = expert_ids.shape[1]
    experts = lax.axis_size("dev")
    capacity = min(tok_count, 2 * tok_count * topk_count // experts)
    slot_count = experts * capacity
    expert_iota = jnp.arange(experts, dtype=jnp.int32)
    named = expert_ids[:, :, None] == expert_iota[None, None, :]
    row_iota = jnp.arange(tok_count, dtype=jnp.int32)
    lower = (row_iota[:, None] > row_iota[None, :]).astype(jnp.bfloat16)
    earlier = jnp.dot(lower, jnp.any(named, axis=1).astype(jnp.bfloat16), preferred_element_type=jnp.float32)
    slot_index = jnp.sum(jnp.where(named, earlier[:, None, :], 0.0), axis=2).astype(jnp.int32)
    destination = expert_ids * capacity + slot_index
    slot_iota = jnp.arange(slot_count, dtype=jnp.int32)
    picks = destination[:, :, None] == slot_iota[None, None, :]
    dispatch = jnp.any(
        destination[None, :, :] == slot_iota[:, None, None], axis=2
    )
    outgoing = jnp.dot(
        dispatch.astype(jnp.bfloat16), moe_rows, preferred_element_type=jnp.float32
    ).astype(jnp.bfloat16).reshape(experts, capacity, width)
    arrived = lax.all_to_all(outgoing, "dev", split_axis=0, concat_axis=0, tiled=True)
    own_rows = arrived.reshape(experts * capacity, width)
    expert_sum = full_expert(own_rows, w_gate, w_up, w_down)
    finished = expert_sum.reshape(experts, capacity, width)
    returned = lax.all_to_all(finished, "dev", split_axis=0, concat_axis=0, tiled=True)
    flat_back = returned.reshape(slot_count, width)
    weighted = jnp.sum(jnp.where(picks, gate_weights[:, :, None], 0.0), axis=1)
    first = lax.reduce_precision(weighted, exponent_bits=8, mantissa_bits=7)
    rest = weighted - first
    second = lax.reduce_precision(rest, exponent_bits=8, mantissa_bits=7)
    parts = [first, second, rest - second]
    split = jnp.concatenate([part.astype(jnp.bfloat16) for part in parts], axis=0)
    sums = jnp.dot(split, flat_back, preferred_element_type=jnp.float32)
    moe_out = (sums[:tok_count] + sums[tok_count:2 * tok_count] + sums[2 * tok_count:]).astype(jnp.bfloat16)
    attended = jax.vmap(attend_row)(q_latent, q_rope, latent_cache, rope_cache, lengths)
    return (moe_out, attended)


def solution(mesh):
    placed = (
        P(("role", "dev"), None),
        P(("role", "dev"), None),
        P(("role", "dev"), None),
        P("dev", None, "role"),
        P("dev", None, "role"),
        P("dev", None, "role"),
        P(("role", "dev"), None, None),
        P(("role", "dev"), None),
        P(("role", "dev"), None, None),
        P(("role", "dev"), None, None),
        P(("role", "dev")),
    )
    return jax.shard_map(
        per_device,
        mesh=mesh,
        in_specs=placed,
        out_specs=(P(("role", "dev"), None), P(("role", "dev"), None, None)),
        check_vma=False,
    )
```

```python
import jax
import jax.numpy as jnp
from jax import lax
from jax.sharding import PartitionSpec as P
from jax.experimental import pallas as pl
from jax.experimental.pallas import tpu as pltpu
import functools

def gate_up_kernel(x_ref, g_ref, u_ref, h_ref):
    x = x_ref[...]
    gate_part = jnp.dot(x, g_ref[...], preferred_element_type=jnp.float32)
    up_part = jnp.dot(x, u_ref[...], preferred_element_type=jnp.float32)
    h_ref[...] = (jax.nn.silu(gate_part) * up_part).astype(h_ref.dtype)


def down_kernel(h0_ref, h1_ref, d0_ref, d1_ref, o_ref):
    total = None
    for h_ref, d_ref in ((h0_ref, d0_ref), (h1_ref, d1_ref)):
        term = lax.dot_general(
            h_ref[...], d_ref[...], (((1,), (1,)), ((), ())), preferred_element_type=jnp.float32
        )
        total = term if total is None else total + term
    o_ref[...] = total.astype(o_ref.dtype)


def gate_up(rows, gate_matrix, up_matrix, unit_tile=256):
    count, width = rows.shape
    units = gate_matrix.shape[1]
    return pl.pallas_call(
        gate_up_kernel,
        out_shape=jax.ShapeDtypeStruct((count, units), jnp.bfloat16),
        grid=(units // unit_tile,),
        in_specs=[
            pl.BlockSpec((count, width), lambda j: (0, 0)),
            pl.BlockSpec((width, unit_tile), lambda j: (0, j)),
            pl.BlockSpec((width, unit_tile), lambda j: (0, j)),
        ],
        out_specs=pl.BlockSpec((count, unit_tile), lambda j: (0, j)),
        compiler_params=pltpu.CompilerParams(vmem_limit_bytes=48 * 1024 * 1024),
        cost_estimate=pl.CostEstimate(
            flops=4 * count * width * units,
            transcendentals=count * units,
            bytes_accessed=2 * (count * width + 2 * width * units + count * units),
        ),
    )(rows, gate_matrix, up_matrix)


def down(h0, h1, d0, d1, out_tile=512):
    count, units = h0.shape
    width = d0.shape[0]
    return pl.pallas_call(
        down_kernel,
        out_shape=jax.ShapeDtypeStruct((count, width), jnp.bfloat16),
        grid=(width // out_tile,),
        in_specs=[
            pl.BlockSpec((count, units), lambda j: (0, 0)),
            pl.BlockSpec((count, units), lambda j: (0, 0)),
            pl.BlockSpec((out_tile, units), lambda j: (j, 0)),
            pl.BlockSpec((out_tile, units), lambda j: (j, 0)),
        ],
        out_specs=pl.BlockSpec((count, out_tile), lambda j: (0, j)),
        compiler_params=pltpu.CompilerParams(vmem_limit_bytes=48 * 1024 * 1024),
        cost_estimate=pl.CostEstimate(
            flops=4 * count * width * units,
            transcendentals=0,
            bytes_accessed=2 * (count * width + 2 * width * units + 2 * count * units),
        ),
    )(h0, h1, d0, d1)


def other_half(w):
    return lax.ppermute(w, "role", [(0, 1), (1, 0)])


def ffn_kernel(steps, x_ref, go_ref, uo_ref, gt_ref, ut_ref, do_ref, dt_ref, o_ref, h_ref):
    i = pl.program_id(0)
    tile = go_ref.shape[1]
    units = h_ref.shape[1] // 2

    def hidden(g_ref, u_ref, column):
        x = x_ref[...]
        gate_part = jnp.dot(x, g_ref[...], preferred_element_type=jnp.float32)
        up_part = jnp.dot(x, u_ref[...], preferred_element_type=jnp.float32)
        h_ref[:, pl.ds(pl.multiple_of(column, tile), tile)] = (
            jax.nn.silu(gate_part) * up_part
        ).astype(h_ref.dtype)

    @pl.when(i < steps)
    def _():
        hidden(go_ref, uo_ref, i * tile)

    @pl.when((i >= steps) & (i < 2 * steps))
    def _():
        hidden(gt_ref, ut_ref, units + (i - steps) * tile)

    @pl.when(i >= 2 * steps)
    def _():
        total = lax.dot_general(
            h_ref[:, :units], do_ref[...], (((1,), (1,)), ((), ())), preferred_element_type=jnp.float32
        )
        total = total + lax.dot_general(
            h_ref[:, units:], dt_ref[...], (((1,), (1,)), ((), ())), preferred_element_type=jnp.float32
        )
        o_ref[...] = total.astype(o_ref.dtype)


def full_expert(rows, w_gate, w_up, w_down, unit_tile=256, out_tile=1792):
    count, width = rows.shape
    own = (w_gate[0], w_up[0], w_down[0])
    other = tuple(other_half(w) for w in own)
    units = own[0].shape[1]
    steps = units // unit_tile
    outs = width // out_tile

    def own_map(i):
        return (0, jnp.minimum(i, steps - 1))

    def other_map(i):
        return (0, jnp.clip(i - steps, 0, steps - 1))

    def down_map(i):
        return (jnp.clip(i - 2 * steps, 0, outs - 1), 0)

    unit_block = (width, unit_tile)
    return pl.pallas_call(
        functools.partial(ffn_kernel, steps),
        out_shape=jax.ShapeDtypeStruct((count, width), jnp.bfloat16),
        grid=(2 * steps + outs,),
        in_specs=[
            pl.BlockSpec((count, width), lambda i: (0, 0)),
            pl.BlockSpec(unit_block, own_map),
            pl.BlockSpec(unit_block, own_map),
            pl.BlockSpec(unit_block, other_map),
            pl.BlockSpec(unit_block, other_map),
            pl.BlockSpec((out_tile, units), down_map),
            pl.BlockSpec((out_tile, units), down_map),
        ],
        out_specs=pl.BlockSpec((count, out_tile), lambda i: (0, jnp.clip(i - 2 * steps, 0, outs - 1))),
        scratch_shapes=[pltpu.VMEM((count, 2 * units), jnp.bfloat16)],
        compiler_params=pltpu.CompilerParams(vmem_limit_bytes=56 * 1024 * 1024),
        cost_estimate=pl.CostEstimate(
            flops=12 * count * width * units,
            transcendentals=2 * count * units,
            bytes_accessed=2 * (2 * count * width + 6 * width * units),
        ),
    )(rows, own[0], own[1], other[0], other[1], own[2], other[2])


score_scale = 192.0 ** (-0.5)


def attend_row(query_lat, query_rope, cache_lat, cache_rope, length):
    head_count = query_lat.shape[0]
    rope_width = cache_rope.shape[0]
    scores = lax.dot_general(
        query_lat, cache_lat, (((1,), (1,)), ((), ())), preferred_element_type=jnp.float32
    )
    scores = scores + jnp.dot(
        query_rope.reshape(head_count, rope_width), cache_rope, preferred_element_type=jnp.float32
    )
    scores = scores * score_scale
    positions = jnp.arange(cache_lat.shape[0], dtype=jnp.int32)
    valid = (positions < length)[None, :]
    scores = jnp.where(valid, scores, jnp.float32(-1e30))
    highest = jnp.max(scores, axis=1, keepdims=True)
    weights = jnp.where(valid, jnp.exp(scores - highest), jnp.float32(0.0))
    probs = (weights / jnp.sum(weights, axis=1, keepdims=True)).astype(jnp.bfloat16)
    return jnp.dot(probs, cache_lat, preferred_element_type=jnp.float32).astype(jnp.bfloat16)


def per_device(
    moe_rows,
    expert_ids,
    gate_weights,
    w_gate,
    w_up,
    w_down,
    q_latent,
    q_rope,
    latent_cache,
    rope_cache,
    lengths,
):
    tok_count = moe_rows.shape[0]
    width = moe_rows.shape[1]
    topk_count = expert_ids.shape[1]
    experts = lax.axis_size("dev")
    capacity = min(tok_count, 2 * tok_count * topk_count // experts)
    slot_count = experts * capacity
    expert_iota = jnp.arange(experts, dtype=jnp.int32)
    ids_t = expert_ids.T
    named = ids_t[:, :, None] == expert_iota[None, None, :]
    row_iota = jnp.arange(tok_count, dtype=jnp.int32)
    lower = (row_iota[:, None] > row_iota[None, :]).astype(jnp.bfloat16)
    earlier = jnp.dot(lower, jnp.any(named, axis=0).astype(jnp.bfloat16), preferred_element_type=jnp.float32)
    slot_index = jnp.sum(jnp.where(named, earlier[None, :, :], 0.0), axis=2).astype(jnp.int32)
    destination = ids_t * capacity + slot_index
    slot_iota = jnp.arange(slot_count, dtype=jnp.int32)
    picks = destination[:, :, None] == slot_iota[None, None, :]
    dispatch = jnp.any(destination[None, :, :] == slot_iota[:, None, None], axis=1)
    outgoing = jnp.dot(
        dispatch.astype(jnp.bfloat16), moe_rows, preferred_element_type=jnp.float32
    ).astype(jnp.bfloat16).reshape(experts, capacity, width)
    arrived = lax.all_to_all(outgoing, "dev", split_axis=0, concat_axis=0, tiled=True)
    own_rows = arrived.reshape(experts * capacity, width)
    expert_sum = full_expert(own_rows, w_gate, w_up, w_down)
    finished = expert_sum.reshape(experts, capacity, width)
    returned = lax.all_to_all(finished, "dev", split_axis=0, concat_axis=0, tiled=True)
    flat_back = returned.reshape(slot_count, width)
    weighted = jnp.sum(jnp.where(picks, gate_weights.T[:, :, None], 0.0), axis=0)
    first = lax.reduce_precision(weighted, exponent_bits=8, mantissa_bits=7)
    rest = weighted - first
    second = lax.reduce_precision(rest, exponent_bits=8, mantissa_bits=7)
    parts = [first, second, rest - second]
    split = jnp.concatenate([part.astype(jnp.bfloat16) for part in parts], axis=0)
    sums = jnp.dot(split, flat_back, preferred_element_type=jnp.float32)
    moe_out = (sums[:tok_count] + sums[tok_count:2 * tok_count] + sums[2 * tok_count:]).astype(jnp.bfloat16)
    attended = jax.vmap(attend_row)(q_latent, q_rope, latent_cache, rope_cache, lengths)
    return (moe_out, attended)


def solution(mesh):
    placed = (
        P(("role", "dev"), None),
        P(("role", "dev"), None),
        P(("role", "dev"), None),
        P("dev", None, "role"),
        P("dev", None, "role"),
        P("dev", None, "role"),
        P(("role", "dev"), None, None),
        P(("role", "dev"), None),
        P(("role", "dev"), None, None),
        P(("role", "dev"), None, None),
        P(("role", "dev")),
    )
    return jax.shard_map(
        per_device,
        mesh=mesh,
        in_specs=placed,
        out_specs=(P(("role", "dev"), None), P(("role", "dev"), None, None)),
        check_vma=False,
    )
```

```python
import jax
import jax.numpy as jnp
from jax import lax
from jax.sharding import PartitionSpec as P
from jax.experimental import pallas as pl
from jax.experimental.pallas import tpu as pltpu
import functools

def gate_up_kernel(x_ref, g_ref, u_ref, h_ref):
    x = x_ref[...]
    gate_part = jnp.dot(x, g_ref[...], preferred_element_type=jnp.float32)
    up_part = jnp.dot(x, u_ref[...], preferred_element_type=jnp.float32)
    h_ref[...] = (jax.nn.silu(gate_part) * up_part).astype(h_ref.dtype)


def down_kernel(h0_ref, h1_ref, d0_ref, d1_ref, o_ref):
    total = None
    for h_ref, d_ref in ((h0_ref, d0_ref), (h1_ref, d1_ref)):
        term = lax.dot_general(
            h_ref[...], d_ref[...], (((1,), (1,)), ((), ())), preferred_element_type=jnp.float32
        )
        total = term if total is None else total + term
    o_ref[...] = total.astype(o_ref.dtype)


def gate_up(rows, gate_matrix, up_matrix, unit_tile=256):
    count, width = rows.shape
    units = gate_matrix.shape[1]
    return pl.pallas_call(
        gate_up_kernel,
        out_shape=jax.ShapeDtypeStruct((count, units), jnp.bfloat16),
        grid=(units // unit_tile,),
        in_specs=[
            pl.BlockSpec((count, width), lambda j: (0, 0)),
            pl.BlockSpec((width, unit_tile), lambda j: (0, j)),
            pl.BlockSpec((width, unit_tile), lambda j: (0, j)),
        ],
        out_specs=pl.BlockSpec((count, unit_tile), lambda j: (0, j)),
        compiler_params=pltpu.CompilerParams(vmem_limit_bytes=48 * 1024 * 1024),
        cost_estimate=pl.CostEstimate(
            flops=4 * count * width * units,
            transcendentals=count * units,
            bytes_accessed=2 * (count * width + 2 * width * units + count * units),
        ),
    )(rows, gate_matrix, up_matrix)


def down(h0, h1, d0, d1, out_tile=512):
    count, units = h0.shape
    width = d0.shape[0]
    return pl.pallas_call(
        down_kernel,
        out_shape=jax.ShapeDtypeStruct((count, width), jnp.bfloat16),
        grid=(width // out_tile,),
        in_specs=[
            pl.BlockSpec((count, units), lambda j: (0, 0)),
            pl.BlockSpec((count, units), lambda j: (0, 0)),
            pl.BlockSpec((out_tile, units), lambda j: (j, 0)),
            pl.BlockSpec((out_tile, units), lambda j: (j, 0)),
        ],
        out_specs=pl.BlockSpec((count, out_tile), lambda j: (0, j)),
        compiler_params=pltpu.CompilerParams(vmem_limit_bytes=48 * 1024 * 1024),
        cost_estimate=pl.CostEstimate(
            flops=4 * count * width * units,
            transcendentals=0,
            bytes_accessed=2 * (count * width + 2 * width * units + 2 * count * units),
        ),
    )(h0, h1, d0, d1)


def other_half(w):
    return lax.ppermute(w, "role", [(0, 1), (1, 0)])


def ffn_kernel(steps, x_ref, go_ref, uo_ref, gt_ref, ut_ref, do_ref, dt_ref, o_ref, h_ref):
    i = pl.program_id(0)
    tile = go_ref.shape[1]
    units = h_ref.shape[1] // 2

    def hidden(g_ref, u_ref, column):
        x = x_ref[...]
        gate_part = jnp.dot(x, g_ref[...], preferred_element_type=jnp.float32)
        up_part = jnp.dot(x, u_ref[...], preferred_element_type=jnp.float32)
        h_ref[:, pl.ds(pl.multiple_of(column, tile), tile)] = (
            jax.nn.silu(gate_part) * up_part
        ).astype(h_ref.dtype)

    @pl.when(i < steps)
    def _():
        hidden(go_ref, uo_ref, i * tile)

    @pl.when((i >= steps) & (i < 2 * steps))
    def _():
        hidden(gt_ref, ut_ref, units + (i - steps) * tile)

    @pl.when(i >= 2 * steps)
    def _():
        total = lax.dot_general(
            h_ref[:, :units], do_ref[...], (((1,), (1,)), ((), ())), preferred_element_type=jnp.float32
        )
        total = total + lax.dot_general(
            h_ref[:, units:], dt_ref[...], (((1,), (1,)), ((), ())), preferred_element_type=jnp.float32
        )
        o_ref[...] = total.astype(o_ref.dtype)


def full_expert(rows, w_gate, w_up, w_down, unit_tile=256, out_tile=1792):
    count, width = rows.shape
    own = (w_gate[0], w_up[0], w_down[0])
    other = tuple(other_half(w) for w in own)
    units = own[0].shape[1]
    steps = units // unit_tile
    outs = width // out_tile

    def own_map(i):
        return (0, jnp.minimum(i, steps - 1))

    def other_map(i):
        return (0, jnp.clip(i - steps, 0, steps - 1))

    def down_map(i):
        return (jnp.clip(i - 2 * steps, 0, outs - 1), 0)

    unit_block = (width, unit_tile)
    return pl.pallas_call(
        functools.partial(ffn_kernel, steps),
        out_shape=jax.ShapeDtypeStruct((count, width), jnp.bfloat16),
        grid=(2 * steps + outs,),
        in_specs=[
            pl.BlockSpec((count, width), lambda i: (0, 0)),
            pl.BlockSpec(unit_block, own_map),
            pl.BlockSpec(unit_block, own_map),
            pl.BlockSpec(unit_block, other_map),
            pl.BlockSpec(unit_block, other_map),
            pl.BlockSpec((out_tile, units), down_map),
            pl.BlockSpec((out_tile, units), down_map),
        ],
        out_specs=pl.BlockSpec((count, out_tile), lambda i: (0, jnp.clip(i - 2 * steps, 0, outs - 1))),
        scratch_shapes=[pltpu.VMEM((count, 2 * units), jnp.bfloat16)],
        compiler_params=pltpu.CompilerParams(vmem_limit_bytes=40 * 1024 * 1024),
        cost_estimate=pl.CostEstimate(
            flops=12 * count * width * units,
            transcendentals=2 * count * units,
            bytes_accessed=2 * (2 * count * width + 6 * width * units),
        ),
    )(rows, own[0], own[1], other[0], other[1], own[2], other[2])


score_scale = 192.0 ** (-0.5)


def attend_row(query_lat, query_rope, cache_lat, cache_rope, length):
    head_count = query_lat.shape[0]
    rope_width = cache_rope.shape[0]
    scores = lax.dot_general(
        query_lat, cache_lat, (((1,), (1,)), ((), ())), preferred_element_type=jnp.float32
    )
    scores = scores + jnp.dot(
        query_rope.reshape(head_count, rope_width), cache_rope, preferred_element_type=jnp.float32
    )
    scores = scores * score_scale
    positions = jnp.arange(cache_lat.shape[0], dtype=jnp.int32)
    valid = (positions < length)[None, :]
    scores = jnp.where(valid, scores, jnp.float32(-1e30))
    highest = jnp.max(scores, axis=1, keepdims=True)
    weights = jnp.where(valid, jnp.exp(scores - highest), jnp.float32(0.0))
    probs = (weights / jnp.sum(weights, axis=1, keepdims=True)).astype(jnp.bfloat16)
    return jnp.dot(probs, cache_lat, preferred_element_type=jnp.float32).astype(jnp.bfloat16)


def per_device(
    moe_rows,
    expert_ids,
    gate_weights,
    w_gate,
    w_up,
    w_down,
    q_latent,
    q_rope,
    latent_cache,
    rope_cache,
    lengths,
):
    tok_count = moe_rows.shape[0]
    width = moe_rows.shape[1]
    topk_count = expert_ids.shape[1]
    experts = lax.axis_size("dev")
    capacity = min(tok_count, 2 * tok_count * topk_count // experts)
    slot_count = experts * capacity
    expert_iota = jnp.arange(experts, dtype=jnp.int32)
    named = expert_ids[:, :, None] == expert_iota[None, None, :]
    row_iota = jnp.arange(tok_count, dtype=jnp.int32)
    lower = (row_iota[:, None] > row_iota[None, :]).astype(jnp.bfloat16)
    earlier = jnp.dot(lower, jnp.any(named, axis=1).astype(jnp.bfloat16), preferred_element_type=jnp.float32)
    slot_index = jnp.sum(jnp.where(named, earlier[:, None, :], 0.0), axis=2).astype(jnp.int32)
    destination = expert_ids * capacity + slot_index
    slot_iota = jnp.arange(slot_count, dtype=jnp.int32)
    picks = destination[:, :, None] == slot_iota[None, None, :]
    dispatch = jnp.any(
        destination[None, :, :] == slot_iota[:, None, None], axis=2
    )
    outgoing = jnp.dot(
        dispatch.astype(jnp.bfloat16), moe_rows, preferred_element_type=jnp.float32
    ).astype(jnp.bfloat16).reshape(experts, capacity, width)
    arrived = lax.all_to_all(outgoing, "dev", split_axis=0, concat_axis=0, tiled=True)
    own_rows = arrived.reshape(experts * capacity, width)
    expert_sum = full_expert(own_rows, w_gate, w_up, w_down)
    finished = expert_sum.reshape(experts, capacity, width)
    returned = lax.all_to_all(finished, "dev", split_axis=0, concat_axis=0, tiled=True)
    flat_back = returned.reshape(slot_count, width)
    weighted = jnp.sum(jnp.where(picks, gate_weights[:, :, None], 0.0), axis=1)
    first = lax.reduce_precision(weighted, exponent_bits=8, mantissa_bits=7)
    rest = weighted - first
    second = lax.reduce_precision(rest, exponent_bits=8, mantissa_bits=7)
    parts = [first, second, rest - second]
    split = jnp.concatenate([part.astype(jnp.bfloat16) for part in parts], axis=0)
    sums = jnp.dot(split, flat_back, preferred_element_type=jnp.float32)
    moe_out = (sums[:tok_count] + sums[tok_count:2 * tok_count] + sums[2 * tok_count:]).astype(jnp.bfloat16)
    attended = jax.vmap(attend_row)(q_latent, q_rope, latent_cache, rope_cache, lengths)
    return (moe_out, attended)


def solution(mesh):
    placed = (
        P(("role", "dev"), None),
        P(("role", "dev"), None),
        P(("role", "dev"), None),
        P("dev", None, "role"),
        P("dev", None, "role"),
        P("dev", None, "role"),
        P(("role", "dev"), None, None),
        P(("role", "dev"), None),
        P(("role", "dev"), None, None),
        P(("role", "dev"), None, None),
        P(("role", "dev")),
    )
    return jax.shard_map(
        per_device,
        mesh=mesh,
        in_specs=placed,
        out_specs=(P(("role", "dev"), None), P(("role", "dev"), None, None)),
        check_vma=False,
    )
```

```python
import jax
import jax.numpy as jnp
from jax import lax
from jax.sharding import PartitionSpec as P
from jax.experimental import pallas as pl
from jax.experimental.pallas import tpu as pltpu
import functools

def gate_up_kernel(x_ref, g_ref, u_ref, h_ref):
    x = x_ref[...]
    gate_part = jnp.dot(x, g_ref[...], preferred_element_type=jnp.float32)
    up_part = jnp.dot(x, u_ref[...], preferred_element_type=jnp.float32)
    h_ref[...] = (jax.nn.silu(gate_part) * up_part).astype(h_ref.dtype)


def down_kernel(h0_ref, h1_ref, d0_ref, d1_ref, o_ref):
    total = None
    for h_ref, d_ref in ((h0_ref, d0_ref), (h1_ref, d1_ref)):
        term = lax.dot_general(
            h_ref[...], d_ref[...], (((1,), (1,)), ((), ())), preferred_element_type=jnp.float32
        )
        total = term if total is None else total + term
    o_ref[...] = total.astype(o_ref.dtype)


def gate_up(rows, gate_matrix, up_matrix, unit_tile=256):
    count, width = rows.shape
    units = gate_matrix.shape[1]
    return pl.pallas_call(
        gate_up_kernel,
        out_shape=jax.ShapeDtypeStruct((count, units), jnp.bfloat16),
        grid=(units // unit_tile,),
        in_specs=[
            pl.BlockSpec((count, width), lambda j: (0, 0)),
            pl.BlockSpec((width, unit_tile), lambda j: (0, j)),
            pl.BlockSpec((width, unit_tile), lambda j: (0, j)),
        ],
        out_specs=pl.BlockSpec((count, unit_tile), lambda j: (0, j)),
        compiler_params=pltpu.CompilerParams(vmem_limit_bytes=48 * 1024 * 1024),
        cost_estimate=pl.CostEstimate(
            flops=4 * count * width * units,
            transcendentals=count * units,
            bytes_accessed=2 * (count * width + 2 * width * units + count * units),
        ),
    )(rows, gate_matrix, up_matrix)


def down(h0, h1, d0, d1, out_tile=512):
    count, units = h0.shape
    width = d0.shape[0]
    return pl.pallas_call(
        down_kernel,
        out_shape=jax.ShapeDtypeStruct((count, width), jnp.bfloat16),
        grid=(width // out_tile,),
        in_specs=[
            pl.BlockSpec((count, units), lambda j: (0, 0)),
            pl.BlockSpec((count, units), lambda j: (0, 0)),
            pl.BlockSpec((out_tile, units), lambda j: (j, 0)),
            pl.BlockSpec((out_tile, units), lambda j: (j, 0)),
        ],
        out_specs=pl.BlockSpec((count, out_tile), lambda j: (0, j)),
        compiler_params=pltpu.CompilerParams(vmem_limit_bytes=48 * 1024 * 1024),
        cost_estimate=pl.CostEstimate(
            flops=4 * count * width * units,
            transcendentals=0,
            bytes_accessed=2 * (count * width + 2 * width * units + 2 * count * units),
        ),
    )(h0, h1, d0, d1)


def other_half(w):
    return lax.ppermute(w, "role", [(0, 1), (1, 0)])


def ffn_kernel(steps, x_ref, go_ref, uo_ref, gt_ref, ut_ref, do_ref, dt_ref, o_ref, h_ref):
    i = pl.program_id(0)
    tile = go_ref.shape[1]
    units = h_ref.shape[1] // 2

    def hidden(g_ref, u_ref, column):
        x = x_ref[...]
        gate_part = jnp.dot(x, g_ref[...], preferred_element_type=jnp.float32)
        up_part = jnp.dot(x, u_ref[...], preferred_element_type=jnp.float32)
        h_ref[:, pl.ds(pl.multiple_of(column, tile), tile)] = (
            jax.nn.silu(gate_part) * up_part
        ).astype(h_ref.dtype)

    @pl.when(i < steps)
    def _():
        hidden(go_ref, uo_ref, i * tile)

    @pl.when((i >= steps) & (i < 2 * steps))
    def _():
        hidden(gt_ref, ut_ref, units + (i - steps) * tile)

    @pl.when(i >= 2 * steps)
    def _():
        total = lax.dot_general(
            h_ref[:, :units], do_ref[...], (((1,), (1,)), ((), ())), preferred_element_type=jnp.float32
        )
        total = total + lax.dot_general(
            h_ref[:, units:], dt_ref[...], (((1,), (1,)), ((), ())), preferred_element_type=jnp.float32
        )
        o_ref[...] = total.astype(o_ref.dtype)


def full_expert(rows, w_gate, w_up, w_down, unit_tile=256, out_tile=1792):
    count, width = rows.shape
    own = (w_gate[0], w_up[0], w_down[0])
    other = tuple(other_half(w) for w in own)
    units = own[0].shape[1]
    steps = units // unit_tile
    outs = width // out_tile

    def own_map(i):
        return (0, jnp.minimum(i, steps - 1))

    def other_map(i):
        return (0, jnp.clip(i - steps, 0, steps - 1))

    def down_map(i):
        return (jnp.clip(i - 2 * steps, 0, outs - 1), 0)

    unit_block = (width, unit_tile)
    return pl.pallas_call(
        functools.partial(ffn_kernel, steps),
        out_shape=jax.ShapeDtypeStruct((count, width), jnp.bfloat16),
        grid=(2 * steps + outs,),
        in_specs=[
            pl.BlockSpec((count, width), lambda i: (0, 0), pipeline_mode=pl.Buffered(1)),
            pl.BlockSpec(unit_block, own_map),
            pl.BlockSpec(unit_block, own_map),
            pl.BlockSpec(unit_block, other_map),
            pl.BlockSpec(unit_block, other_map),
            pl.BlockSpec((out_tile, units), down_map),
            pl.BlockSpec((out_tile, units), down_map),
        ],
        out_specs=pl.BlockSpec((count, out_tile), lambda i: (0, jnp.clip(i - 2 * steps, 0, outs - 1))),
        scratch_shapes=[pltpu.VMEM((count, 2 * units), jnp.bfloat16)],
        compiler_params=pltpu.CompilerParams(vmem_limit_bytes=36 * 1024 * 1024),
        cost_estimate=pl.CostEstimate(
            flops=12 * count * width * units,
            transcendentals=2 * count * units,
            bytes_accessed=2 * (2 * count * width + 6 * width * units),
        ),
    )(rows, own[0], own[1], other[0], other[1], own[2], other[2])


score_scale = 192.0 ** (-0.5)


def attend_row(query_lat, query_rope, cache_lat, cache_rope, length):
    head_count = query_lat.shape[0]
    rope_width = cache_rope.shape[0]
    scores = lax.dot_general(
        query_lat, cache_lat, (((1,), (1,)), ((), ())), preferred_element_type=jnp.float32
    )
    scores = scores + jnp.dot(
        query_rope.reshape(head_count, rope_width), cache_rope, preferred_element_type=jnp.float32
    )
    scores = scores * score_scale
    positions = jnp.arange(cache_lat.shape[0], dtype=jnp.int32)
    valid = (positions < length)[None, :]
    scores = jnp.where(valid, scores, jnp.float32(-1e30))
    highest = jnp.max(scores, axis=1, keepdims=True)
    weights = jnp.where(valid, jnp.exp(scores - highest), jnp.float32(0.0))
    probs = (weights / jnp.sum(weights, axis=1, keepdims=True)).astype(jnp.bfloat16)
    return jnp.dot(probs, cache_lat, preferred_element_type=jnp.float32).astype(jnp.bfloat16)


def per_device(
    moe_rows,
    expert_ids,
    gate_weights,
    w_gate,
    w_up,
    w_down,
    q_latent,
    q_rope,
    latent_cache,
    rope_cache,
    lengths,
):
    tok_count = moe_rows.shape[0]
    width = moe_rows.shape[1]
    topk_count = expert_ids.shape[1]
    experts = lax.axis_size("dev")
    capacity = min(tok_count, 2 * tok_count * topk_count // experts)
    slot_count = experts * capacity
    expert_iota = jnp.arange(experts, dtype=jnp.int32)
    named = expert_ids[:, :, None] == expert_iota[None, None, :]
    row_iota = jnp.arange(tok_count, dtype=jnp.int32)
    lower = (row_iota[:, None] > row_iota[None, :]).astype(jnp.bfloat16)
    earlier = jnp.dot(lower, jnp.any(named, axis=1).astype(jnp.bfloat16), preferred_element_type=jnp.float32)
    slot_index = jnp.sum(jnp.where(named, earlier[:, None, :], 0.0), axis=2).astype(jnp.int32)
    destination = expert_ids * capacity + slot_index
    slot_iota = jnp.arange(slot_count, dtype=jnp.int32)
    picks = destination[:, :, None] == slot_iota[None, None, :]
    dispatch = jnp.any(
        destination[None, :, :] == slot_iota[:, None, None], axis=2
    )
    outgoing = jnp.dot(
        dispatch.astype(jnp.bfloat16), moe_rows, preferred_element_type=jnp.float32
    ).astype(jnp.bfloat16).reshape(experts, capacity, width)
    arrived = lax.all_to_all(outgoing, "dev", split_axis=0, concat_axis=0, tiled=True)
    own_rows = arrived.reshape(experts * capacity, width)
    expert_sum = full_expert(own_rows, w_gate, w_up, w_down)
    finished = expert_sum.reshape(experts, capacity, width)
    returned = lax.all_to_all(finished, "dev", split_axis=0, concat_axis=0, tiled=True)
    flat_back = returned.reshape(slot_count, width)
    weighted = jnp.sum(jnp.where(picks, gate_weights[:, :, None], 0.0), axis=1)
    first = lax.reduce_precision(weighted, exponent_bits=8, mantissa_bits=7)
    rest = weighted - first
    second = lax.reduce_precision(rest, exponent_bits=8, mantissa_bits=7)
    parts = [first, second, rest - second]
    split = jnp.concatenate([part.astype(jnp.bfloat16) for part in parts], axis=0)
    sums = jnp.dot(split, flat_back, preferred_element_type=jnp.float32)
    moe_out = (sums[:tok_count] + sums[tok_count:2 * tok_count] + sums[2 * tok_count:]).astype(jnp.bfloat16)
    attended = jax.vmap(attend_row)(q_latent, q_rope, latent_cache, rope_cache, lengths)
    return (moe_out, attended)


def solution(mesh):
    placed = (
        P(("role", "dev"), None),
        P(("role", "dev"), None),
        P(("role", "dev"), None),
        P("dev", None, "role"),
        P("dev", None, "role"),
        P("dev", None, "role"),
        P(("role", "dev"), None, None),
        P(("role", "dev"), None),
        P(("role", "dev"), None, None),
        P(("role", "dev"), None, None),
        P(("role", "dev")),
    )
    return jax.shard_map(
        per_device,
        mesh=mesh,
        in_specs=placed,
        out_specs=(P(("role", "dev"), None), P(("role", "dev"), None, None)),
        check_vma=False,
    )
```

```python
import jax
import jax.numpy as jnp
from jax import lax
from jax.sharding import PartitionSpec as P
from jax.experimental import pallas as pl
from jax.experimental.pallas import tpu as pltpu
import functools

def gate_up_kernel(x_ref, g_ref, u_ref, h_ref):
    x = x_ref[...]
    gate_part = jnp.dot(x, g_ref[...], preferred_element_type=jnp.float32)
    up_part = jnp.dot(x, u_ref[...], preferred_element_type=jnp.float32)
    h_ref[...] = (jax.nn.silu(gate_part) * up_part).astype(h_ref.dtype)


def down_kernel(h0_ref, h1_ref, d0_ref, d1_ref, o_ref):
    total = None
    for h_ref, d_ref in ((h0_ref, d0_ref), (h1_ref, d1_ref)):
        term = lax.dot_general(
            h_ref[...], d_ref[...], (((1,), (1,)), ((), ())), preferred_element_type=jnp.float32
        )
        total = term if total is None else total + term
    o_ref[...] = total.astype(o_ref.dtype)


def gate_up(rows, gate_matrix, up_matrix, unit_tile=256):
    count, width = rows.shape
    units = gate_matrix.shape[1]
    return pl.pallas_call(
        gate_up_kernel,
        out_shape=jax.ShapeDtypeStruct((count, units), jnp.bfloat16),
        grid=(units // unit_tile,),
        in_specs=[
            pl.BlockSpec((count, width), lambda j: (0, 0)),
            pl.BlockSpec((width, unit_tile), lambda j: (0, j)),
            pl.BlockSpec((width, unit_tile), lambda j: (0, j)),
        ],
        out_specs=pl.BlockSpec((count, unit_tile), lambda j: (0, j)),
        compiler_params=pltpu.CompilerParams(vmem_limit_bytes=48 * 1024 * 1024),
        cost_estimate=pl.CostEstimate(
            flops=4 * count * width * units,
            transcendentals=count * units,
            bytes_accessed=2 * (count * width + 2 * width * units + count * units),
        ),
    )(rows, gate_matrix, up_matrix)


def down(h0, h1, d0, d1, out_tile=512):
    count, units = h0.shape
    width = d0.shape[0]
    return pl.pallas_call(
        down_kernel,
        out_shape=jax.ShapeDtypeStruct((count, width), jnp.bfloat16),
        grid=(width // out_tile,),
        in_specs=[
            pl.BlockSpec((count, units), lambda j: (0, 0)),
            pl.BlockSpec((count, units), lambda j: (0, 0)),
            pl.BlockSpec((out_tile, units), lambda j: (j, 0)),
            pl.BlockSpec((out_tile, units), lambda j: (j, 0)),
        ],
        out_specs=pl.BlockSpec((count, out_tile), lambda j: (0, j)),
        compiler_params=pltpu.CompilerParams(vmem_limit_bytes=48 * 1024 * 1024),
        cost_estimate=pl.CostEstimate(
            flops=4 * count * width * units,
            transcendentals=0,
            bytes_accessed=2 * (count * width + 2 * width * units + 2 * count * units),
        ),
    )(h0, h1, d0, d1)


def other_half(w):
    return lax.ppermute(w, "role", [(0, 1), (1, 0)])


def ffn_kernel(steps, x_ref, go_ref, uo_ref, gt_ref, ut_ref, do_ref, dt_ref, o_ref, h_ref):
    i = pl.program_id(0)
    tile = go_ref.shape[1]
    units = h_ref.shape[1] // 2

    def hidden(g_ref, u_ref, column):
        x = x_ref[...]
        gate_part = jnp.dot(x, g_ref[...], preferred_element_type=jnp.float32)
        up_part = jnp.dot(x, u_ref[...], preferred_element_type=jnp.float32)
        h_ref[:, pl.ds(pl.multiple_of(column, tile), tile)] = (
            jax.nn.silu(gate_part) * up_part
        ).astype(h_ref.dtype)

    @pl.when(i < steps)
    def _():
        hidden(go_ref, uo_ref, i * tile)

    @pl.when((i >= steps) & (i < 2 * steps))
    def _():
        hidden(gt_ref, ut_ref, units + (i - steps) * tile)

    @pl.when(i >= 2 * steps)
    def _():
        total = lax.dot_general(
            h_ref[:, :units], do_ref[...], (((1,), (1,)), ((), ())), preferred_element_type=jnp.float32
        )
        total = total + lax.dot_general(
            h_ref[:, units:], dt_ref[...], (((1,), (1,)), ((), ())), preferred_element_type=jnp.float32
        )
        o_ref[...] = total.astype(o_ref.dtype)


def full_expert(rows, w_gate, w_up, w_down, unit_tile=256, out_tile=512):
    count, width = rows.shape
    own = (w_gate[0], w_up[0], w_down[0])
    other = tuple(other_half(w) for w in own)
    units = own[0].shape[1]
    steps = units // unit_tile
    outs = width // out_tile

    def own_map(i):
        return (0, jnp.minimum(i, steps - 1))

    def other_map(i):
        return (0, jnp.clip(i - steps, 0, steps - 1))

    def down_map(i):
        return (jnp.clip(i - 2 * steps, 0, outs - 1), 0)

    unit_block = (width, unit_tile)
    return pl.pallas_call(
        functools.partial(ffn_kernel, steps),
        out_shape=jax.ShapeDtypeStruct((count, width), jnp.bfloat16),
        grid=(2 * steps + outs,),
        in_specs=[
            pl.BlockSpec((count, width), lambda i: (0, 0), pipeline_mode=pl.Buffered(1)),
            pl.BlockSpec(unit_block, own_map),
            pl.BlockSpec(unit_block, own_map),
            pl.BlockSpec(unit_block, other_map),
            pl.BlockSpec(unit_block, other_map),
            pl.BlockSpec((out_tile, units), down_map),
            pl.BlockSpec((out_tile, units), down_map),
        ],
        out_specs=pl.BlockSpec((count, out_tile), lambda i: (0, jnp.clip(i - 2 * steps, 0, outs - 1))),
        scratch_shapes=[pltpu.VMEM((count, 2 * units), jnp.bfloat16)],
        compiler_params=pltpu.CompilerParams(vmem_limit_bytes=36 * 1024 * 1024),
        cost_estimate=pl.CostEstimate(
            flops=12 * count * width * units,
            transcendentals=2 * count * units,
            bytes_accessed=2 * (2 * count * width + 6 * width * units),
        ),
    )(rows, own[0], own[1], other[0], other[1], own[2], other[2])


score_scale = 192.0 ** (-0.5)


def attend_row(query_lat, query_rope, cache_lat, cache_rope, length):
    head_count = query_lat.shape[0]
    rope_width = cache_rope.shape[0]
    scores = lax.dot_general(
        query_lat, cache_lat, (((1,), (1,)), ((), ())), preferred_element_type=jnp.float32
    )
    scores = scores + jnp.dot(
        query_rope.reshape(head_count, rope_width), cache_rope, preferred_element_type=jnp.float32
    )
    scores = scores * score_scale
    positions = jnp.arange(cache_lat.shape[0], dtype=jnp.int32)
    valid = (positions < length)[None, :]
    scores = jnp.where(valid, scores, jnp.float32(-1e30))
    highest = jnp.max(scores, axis=1, keepdims=True)
    weights = jnp.where(valid, jnp.exp(scores - highest), jnp.float32(0.0))
    probs = (weights / jnp.sum(weights, axis=1, keepdims=True)).astype(jnp.bfloat16)
    return jnp.dot(probs, cache_lat, preferred_element_type=jnp.float32).astype(jnp.bfloat16)


def per_device(
    moe_rows,
    expert_ids,
    gate_weights,
    w_gate,
    w_up,
    w_down,
    q_latent,
    q_rope,
    latent_cache,
    rope_cache,
    lengths,
):
    tok_count = moe_rows.shape[0]
    width = moe_rows.shape[1]
    topk_count = expert_ids.shape[1]
    experts = lax.axis_size("dev")
    capacity = min(tok_count, 2 * tok_count * topk_count // experts)
    slot_count = experts * capacity
    expert_iota = jnp.arange(experts, dtype=jnp.int32)
    named = expert_ids[:, :, None] == expert_iota[None, None, :]
    row_iota = jnp.arange(tok_count, dtype=jnp.int32)
    lower = (row_iota[:, None] > row_iota[None, :]).astype(jnp.bfloat16)
    earlier = jnp.dot(lower, jnp.any(named, axis=1).astype(jnp.bfloat16), preferred_element_type=jnp.float32)
    slot_index = jnp.sum(jnp.where(named, earlier[:, None, :], 0.0), axis=2).astype(jnp.int32)
    destination = expert_ids * capacity + slot_index
    slot_iota = jnp.arange(slot_count, dtype=jnp.int32)
    picks = destination[:, :, None] == slot_iota[None, None, :]
    dispatch = jnp.any(
        destination[None, :, :] == slot_iota[:, None, None], axis=2
    )
    outgoing = jnp.dot(
        dispatch.astype(jnp.bfloat16), moe_rows, preferred_element_type=jnp.float32
    ).astype(jnp.bfloat16).reshape(experts, capacity, width)
    arrived = lax.all_to_all(outgoing, "dev", split_axis=0, concat_axis=0, tiled=True)
    own_rows = arrived.reshape(experts * capacity, width)
    expert_sum = full_expert(own_rows, w_gate, w_up, w_down)
    finished = expert_sum.reshape(experts, capacity, width)
    returned = lax.all_to_all(finished, "dev", split_axis=0, concat_axis=0, tiled=True)
    flat_back = returned.reshape(slot_count, width)
    weighted = jnp.sum(jnp.where(picks, gate_weights[:, :, None], 0.0), axis=1)
    first = lax.reduce_precision(weighted, exponent_bits=8, mantissa_bits=7)
    rest = weighted - first
    second = lax.reduce_precision(rest, exponent_bits=8, mantissa_bits=7)
    parts = [first, second, rest - second]
    split = jnp.concatenate([part.astype(jnp.bfloat16) for part in parts], axis=0)
    sums = jnp.dot(split, flat_back, preferred_element_type=jnp.float32)
    moe_out = (sums[:tok_count] + sums[tok_count:2 * tok_count] + sums[2 * tok_count:]).astype(jnp.bfloat16)
    attended = jax.vmap(attend_row)(q_latent, q_rope, latent_cache, rope_cache, lengths)
    return (moe_out, attended)


def solution(mesh):
    placed = (
        P(("role", "dev"), None),
        P(("role", "dev"), None),
        P(("role", "dev"), None),
        P("dev", None, "role"),
        P("dev", None, "role"),
        P("dev", None, "role"),
        P(("role", "dev"), None, None),
        P(("role", "dev"), None),
        P(("role", "dev"), None, None),
        P(("role", "dev"), None, None),
        P(("role", "dev")),
    )
    return jax.shard_map(
        per_device,
        mesh=mesh,
        in_specs=placed,
        out_specs=(P(("role", "dev"), None), P(("role", "dev"), None, None)),
        check_vma=False,
    )
```

```python
import jax
import jax.numpy as jnp
from jax import lax
from jax.sharding import PartitionSpec as P
from jax.experimental import pallas as pl
from jax.experimental.pallas import tpu as pltpu
import functools

def gate_up_kernel(x_ref, g_ref, u_ref, h_ref):
    x = x_ref[...]
    gate_part = jnp.dot(x, g_ref[...], preferred_element_type=jnp.float32)
    up_part = jnp.dot(x, u_ref[...], preferred_element_type=jnp.float32)
    h_ref[...] = (jax.nn.silu(gate_part) * up_part).astype(h_ref.dtype)


def down_kernel(h0_ref, h1_ref, d0_ref, d1_ref, o_ref):
    total = None
    for h_ref, d_ref in ((h0_ref, d0_ref), (h1_ref, d1_ref)):
        term = lax.dot_general(
            h_ref[...], d_ref[...], (((1,), (1,)), ((), ())), preferred_element_type=jnp.float32
        )
        total = term if total is None else total + term
    o_ref[...] = total.astype(o_ref.dtype)


def gate_up(rows, gate_matrix, up_matrix, unit_tile=256):
    count, width = rows.shape
    units = gate_matrix.shape[1]
    return pl.pallas_call(
        gate_up_kernel,
        out_shape=jax.ShapeDtypeStruct((count, units), jnp.bfloat16),
        grid=(units // unit_tile,),
        in_specs=[
            pl.BlockSpec((count, width), lambda j: (0, 0)),
            pl.BlockSpec((width, unit_tile), lambda j: (0, j)),
            pl.BlockSpec((width, unit_tile), lambda j: (0, j)),
        ],
        out_specs=pl.BlockSpec((count, unit_tile), lambda j: (0, j)),
        compiler_params=pltpu.CompilerParams(vmem_limit_bytes=48 * 1024 * 1024),
        cost_estimate=pl.CostEstimate(
            flops=4 * count * width * units,
            transcendentals=count * units,
            bytes_accessed=2 * (count * width + 2 * width * units + count * units),
        ),
    )(rows, gate_matrix, up_matrix)


def down(h0, h1, d0, d1, out_tile=512):
    count, units = h0.shape
    width = d0.shape[0]
    return pl.pallas_call(
        down_kernel,
        out_shape=jax.ShapeDtypeStruct((count, width), jnp.bfloat16),
        grid=(width // out_tile,),
        in_specs=[
            pl.BlockSpec((count, units), lambda j: (0, 0)),
            pl.BlockSpec((count, units), lambda j: (0, 0)),
            pl.BlockSpec((out_tile, units), lambda j: (j, 0)),
            pl.BlockSpec((out_tile, units), lambda j: (j, 0)),
        ],
        out_specs=pl.BlockSpec((count, out_tile), lambda j: (0, j)),
        compiler_params=pltpu.CompilerParams(vmem_limit_bytes=48 * 1024 * 1024),
        cost_estimate=pl.CostEstimate(
            flops=4 * count * width * units,
            transcendentals=0,
            bytes_accessed=2 * (count * width + 2 * width * units + 2 * count * units),
        ),
    )(h0, h1, d0, d1)


def other_half(w):
    return lax.ppermute(w, "role", [(0, 1), (1, 0)])


def ffn_kernel(steps, x_ref, go_ref, uo_ref, gt_ref, ut_ref, do_ref, dt_ref, o_ref, h_ref):
    i = pl.program_id(0)
    tile = go_ref.shape[1]
    units = h_ref.shape[1] // 2

    def hidden(g_ref, u_ref, column):
        x = x_ref[...]
        gate_part = jnp.dot(x, g_ref[...], preferred_element_type=jnp.float32)
        up_part = jnp.dot(x, u_ref[...], preferred_element_type=jnp.float32)
        h_ref[:, pl.ds(pl.multiple_of(column, tile), tile)] = (
            jax.nn.silu(gate_part) * up_part
        ).astype(h_ref.dtype)

    @pl.when(i < steps)
    def _():
        hidden(go_ref, uo_ref, i * tile)

    @pl.when((i >= steps) & (i < 2 * steps))
    def _():
        hidden(gt_ref, ut_ref, units + (i - steps) * tile)

    @pl.when(i >= 2 * steps)
    def _():
        total = lax.dot_general(
            h_ref[:, :units], do_ref[...], (((1,), (1,)), ((), ())), preferred_element_type=jnp.float32
        )
        total = total + lax.dot_general(
            h_ref[:, units:], dt_ref[...], (((1,), (1,)), ((), ())), preferred_element_type=jnp.float32
        )
        o_ref[...] = total.astype(o_ref.dtype)


def full_expert(rows, w_gate, w_up, w_down, unit_tile=256, out_tile=1792):
    count, width = rows.shape
    own = (w_gate[0], w_up[0], w_down[0])
    other = tuple(other_half(w) for w in own)
    units = own[0].shape[1]
    steps = units // unit_tile
    outs = width // out_tile

    def own_map(i):
        return (0, jnp.minimum(i, steps - 1))

    def other_map(i):
        return (0, jnp.clip(i - steps, 0, steps - 1))

    def down_map(i):
        return (jnp.clip(i - 2 * steps, 0, outs - 1), 0)

    unit_block = (width, unit_tile)
    return pl.pallas_call(
        functools.partial(ffn_kernel, steps),
        out_shape=jax.ShapeDtypeStruct((count, width), jnp.bfloat16),
        grid=(2 * steps + outs,),
        in_specs=[
            pl.BlockSpec((count, width), lambda i: (0, 0), pipeline_mode=pl.Buffered(1)),
            pl.BlockSpec(unit_block, own_map),
            pl.BlockSpec(unit_block, own_map),
            pl.BlockSpec(unit_block, other_map),
            pl.BlockSpec(unit_block, other_map),
            pl.BlockSpec((out_tile, units), down_map),
            pl.BlockSpec((out_tile, units), down_map),
        ],
        out_specs=pl.BlockSpec((count, out_tile), lambda i: (0, jnp.clip(i - 2 * steps, 0, outs - 1))),
        scratch_shapes=[pltpu.VMEM((count, 2 * units), jnp.bfloat16)],
        compiler_params=pltpu.CompilerParams(vmem_limit_bytes=28 * 1024 * 1024),
        cost_estimate=pl.CostEstimate(
            flops=12 * count * width * units,
            transcendentals=2 * count * units,
            bytes_accessed=2 * (2 * count * width + 6 * width * units),
        ),
    )(rows, own[0], own[1], other[0], other[1], own[2], other[2])


score_scale = 192.0 ** (-0.5)


def attend_row(query_lat, query_rope, cache_lat, cache_rope, length):
    head_count = query_lat.shape[0]
    rope_width = cache_rope.shape[0]
    scores = lax.dot_general(
        query_lat, cache_lat, (((1,), (1,)), ((), ())), preferred_element_type=jnp.float32
    )
    scores = scores + jnp.dot(
        query_rope.reshape(head_count, rope_width), cache_rope, preferred_element_type=jnp.float32
    )
    scores = scores * score_scale
    positions = jnp.arange(cache_lat.shape[0], dtype=jnp.int32)
    valid = (positions < length)[None, :]
    scores = jnp.where(valid, scores, jnp.float32(-1e30))
    highest = jnp.max(scores, axis=1, keepdims=True)
    weights = jnp.where(valid, jnp.exp(scores - highest), jnp.float32(0.0))
    probs = (weights / jnp.sum(weights, axis=1, keepdims=True)).astype(jnp.bfloat16)
    return jnp.dot(probs, cache_lat, preferred_element_type=jnp.float32).astype(jnp.bfloat16)


def per_device(
    moe_rows,
    expert_ids,
    gate_weights,
    w_gate,
    w_up,
    w_down,
    q_latent,
    q_rope,
    latent_cache,
    rope_cache,
    lengths,
):
    tok_count = moe_rows.shape[0]
    width = moe_rows.shape[1]
    topk_count = expert_ids.shape[1]
    experts = lax.axis_size("dev")
    capacity = min(tok_count, 2 * tok_count * topk_count // experts)
    slot_count = experts * capacity
    expert_iota = jnp.arange(experts, dtype=jnp.int32)
    named = expert_ids[:, :, None] == expert_iota[None, None, :]
    row_iota = jnp.arange(tok_count, dtype=jnp.int32)
    lower = (row_iota[:, None] > row_iota[None, :]).astype(jnp.bfloat16)
    earlier = jnp.dot(lower, jnp.any(named, axis=1).astype(jnp.bfloat16), preferred_element_type=jnp.float32)
    slot_index = jnp.sum(jnp.where(named, earlier[:, None, :], 0.0), axis=2).astype(jnp.int32)
    destination = expert_ids * capacity + slot_index
    slot_iota = jnp.arange(slot_count, dtype=jnp.int32)
    picks = destination[:, :, None] == slot_iota[None, None, :]
    dispatch = jnp.any(
        destination[None, :, :] == slot_iota[:, None, None], axis=2
    )
    outgoing = jnp.dot(
        dispatch.astype(jnp.bfloat16), moe_rows, preferred_element_type=jnp.float32
    ).astype(jnp.bfloat16).reshape(experts, capacity, width)
    arrived = lax.all_to_all(outgoing, "dev", split_axis=0, concat_axis=0, tiled=True)
    own_rows = arrived.reshape(experts * capacity, width)
    expert_sum = full_expert(own_rows, w_gate, w_up, w_down)
    finished = expert_sum.reshape(experts, capacity, width)
    returned = lax.all_to_all(finished, "dev", split_axis=0, concat_axis=0, tiled=True)
    flat_back = returned.reshape(slot_count, width)
    weighted = jnp.sum(jnp.where(picks, gate_weights[:, :, None], 0.0), axis=1)
    first = lax.reduce_precision(weighted, exponent_bits=8, mantissa_bits=7)
    rest = weighted - first
    second = lax.reduce_precision(rest, exponent_bits=8, mantissa_bits=7)
    parts = [first, second, rest - second]
    split = jnp.concatenate([part.astype(jnp.bfloat16) for part in parts], axis=0)
    sums = jnp.dot(split, flat_back, preferred_element_type=jnp.float32)
    moe_out = (sums[:tok_count] + sums[tok_count:2 * tok_count] + sums[2 * tok_count:]).astype(jnp.bfloat16)
    attended = jax.vmap(attend_row)(q_latent, q_rope, latent_cache, rope_cache, lengths)
    return (moe_out, attended)


def solution(mesh):
    placed = (
        P(("role", "dev"), None),
        P(("role", "dev"), None),
        P(("role", "dev"), None),
        P("dev", None, "role"),
        P("dev", None, "role"),
        P("dev", None, "role"),
        P(("role", "dev"), None, None),
        P(("role", "dev"), None),
        P(("role", "dev"), None, None),
        P(("role", "dev"), None, None),
        P(("role", "dev")),
    )
    return jax.shard_map(
        per_device,
        mesh=mesh,
        in_specs=placed,
        out_specs=(P(("role", "dev"), None), P(("role", "dev"), None, None)),
        check_vma=False,
    )
```
